128 devices in a mesh: tp: 4 (over x), ep: 32 (over z, y, core).
Axes of the slice: x: 4, y: 4, z: 4, core: 2. Of those that a mesh axis runs over, the one named last changes fastest.
Arguments:
- tokens: bfloat16 [4096, 5120], P('ep', 'tp'), may hold values from -6 to 6
- cotangent: bfloat16 [4096, 5120], P('ep', 'tp'), may hold values from -6 to 6
- expert_ids: int32 [4096, 3], P('ep'), may hold values from 0 to 31, all different within a row; in each aligned block of 128 rows (0 to 127, 128 to 255, ...) at most 15 rows name the same one
- gate_weights: float32 [4096, 4], P('ep'), may hold values from 0.1 to 1
- shadow_mask: int32 [4096], P('ep'), may hold values 0 or 1
- w_gate: bfloat16 [32, 5120, 1536], P('ep', None, 'tp'), may hold values from -0.078125 to 0.078125
- w_up: bfloat16 [32, 5120, 1536], P('ep', None, 'tp'), may hold values from -0.078125 to 0.078125
- w_down: bfloat16 [32, 1536, 5120], P('ep', 'tp'), may hold values from -0.15625 to 0.15625
- s_gate: bfloat16 [5120, 1536], P('ep', 'tp'), may hold values from -0.078125 to 0.078125
- s_up: bfloat16 [5120, 1536], P('ep', 'tp'), may hold values from -0.078125 to 0.078125
- s_down: bfloat16 [1536, 5120], P('tp', 'ep'), may hold values from -0.15625 to 0.15625
Outputs:
- mixed: bfloat16 [4096, 5120], P('ep', 'tp')
- grad_gate: bfloat16 [32, 5120, 1536], P('ep', None, 'tp')
- grad_up: bfloat16 [32, 5120, 1536], P('ep', None, 'tp')
- grad_down: bfloat16 [32, 1536, 5120], P('ep', 'tp')
- grad_s_gate: bfloat16 [5120, 1536], P('ep', 'tp')
- grad_s_up: bfloat16 [5120, 1536], P('ep', 'tp')
- grad_s_down: bfloat16 [1536, 5120], P('tp', 'ep')
The draws below stay inside these ranges and needn't reach their ends.
Inputs may be any that keep to these rules, and one draw needn't show every extreme that they name: `expert_ids`: each row names 3 different experts. Among the 128 rows of one device no expert is named more than 15 times, and in every draw some expert is named exactly 15 times by the rows of some device.
All inputs are finite; a program needn't handle non-finite values. No bound on the sum of `shadow_mask` on one device may be relied on, other than what follows from the above.
Results may differ from the reference program's by a relative error of at most 0.028.
Values may be sent and summed in bfloat16 or wider, within the bound.
A program may use at most 192 MiB of HBM per device.

```python
import math
import jax
import jax.numpy as jnp
import numpy as np
from jax import lax

D = 5120
FF = 1536
TOK_DEV = 128
TOP_OLD = 3
EXPERTS = 32
CAP = 15
TOKENS = 4096
N_TP = 4
N_EP = 32


def set_ends(result, rng, low, largest):
    longest = result.shape.index(max(result.shape))
    spots = []
    for shift in (0, 1):
        where = [jax.random.randint(jax.random.fold_in(rng, axis), (), 0, length) for axis, length in enumerate(result.shape)]
        where[longest] = (where[longest] + shift) % result.shape[longest]
        spots.append(tuple(where))
    return result.at[spots[0]].set(low).at[spots[1]].set(largest)


def strengthened(entries, key, source, target, blocks, factor):
    owner, partner = [(jnp.arange(entries.shape[dim]) // (entries.shape[dim] // blocks)).reshape([-1 if axis == dim else 1 for axis in range(entries.ndim)]) for dim in (source, target)]
    chosen = jax.random.permutation(key, blocks)[partner]
    strong = (owner == chosen) | (owner == (partner + blocks // 2) % blocks)
    return jnp.where(strong, factor * entries, entries)


def levels(rng, dims, shards, low, largest):
    def one(axis_at, shards_of):
        draws = jax.random.uniform(jax.random.fold_in(jax.random.fold_in(rng, 6), axis_at), (shards_of,), jnp.float32, low / len(shards), largest / len(shards))
        return jnp.repeat(jnp.exp(draws), dims[axis_at] // shards_of).reshape((-1,) + (1,) * (len(dims) - axis_at - 1))

    gain = one(*shards[0])
    for cut in shards[1:]:
        gain = gain * one(*cut)
    return gain


def assign_block(own_key, own, number, rows, amount, top, bound, lean):
    order = jax.random.permutation(own_key, amount)
    heavy_load, ordinary = load_shares(amount, rows * top, bound, lean, True), load_shares(amount, rows * top, bound, lean, False)
    places = jnp.arange(amount)

    def named(tallies, rotation):
        used = int((tallies > 0).sum())
        fixed = max(1, used // 4)
        moved = fixed + (places - fixed + rotation * (used - fixed)) % max(1, amount - fixed)
        return jnp.zeros((amount,), jnp.int32).at[order[jnp.where(places < fixed, places, moved)]].set(jnp.asarray(tallies, jnp.int32))

    tallies = jnp.where(number % 4 == 0, named(heavy_load, number // 4), named(ordinary, number - number // 4 - 1))
    mixed = jax.random.permutation(jax.random.fold_in(own, 3), amount)
    source_of, receiver = mixed[0:amount // 2 * 2:2], mixed[1:amount // 2 * 2:2]
    slack = jnp.minimum(tallies[source_of] - 1, bound - tallies[receiver]) // 2
    slack = jnp.where((source_of == order[0]) | (receiver == order[0]) | (tallies[receiver] == 0), 0, jnp.maximum(slack, 0))
    moved = jax.random.randint(jax.random.fold_in(own, 4), (amount // 2,), 0, 1 << 20) % (slack + 1)
    tallies = tallies.at[source_of].add(-moved).at[receiver].add(moved)
    labels = jnp.searchsorted(jnp.cumsum(tallies), jnp.arange(rows * top), side="right").astype(jnp.int32)
    table = labels.reshape(top, rows).T
    table = table[jax.random.permutation(jax.random.fold_in(own, 1), rows)]
    rotation = jax.random.randint(jax.random.fold_in(own, 2), (rows, 1), 0, top)
    return jnp.take_along_axis(table, (jnp.arange(top)[None, :] + rotation) % top, axis=1)


def load_shares(number_of, total, most, skew, full):
    loads = [(1 << 20) // math.isqrt(rank ** skew) + 1 for rank in range(1, number_of + 1)]
    largest = most if full else min(most, max(-(-total // number_of), total * loads[0] // sum(loads)))
    least = 1 if total - largest >= number_of - 1 else 0
    counts, rest = [largest] + [least] * (number_of - 1), total - largest - least * (number_of - 1)
    while rest > 0:
        movable = [i for i in range(1, number_of) if counts[i] < largest] or [i for i in range(1, number_of) if counts[i] < most]
        mass, left = sum([loads[i] for i in movable]), rest
        for i in movable:
            extra = min(most - counts[i], max(1, left * loads[i] // mass), rest)
            counts[i] = counts[i] + extra
            rest = rest - extra
    return np.array(counts)


def noise(stream_key, dims, scale, most, pieces=(), held_as=jnp.bfloat16):
    entries = jax.random.normal(stream_key, dims, jnp.float32) * scale
    if len(pieces) > 0:
        entries = levels(stream_key, dims, pieces, -0.22, 0.18) * entries
    return jnp.clip(entries, min=-most, max=most).astype(held_as)


def bell_draw_with(stream_key, extent, spread, reach, shards, heavy, kind=jnp.bfloat16):
    entries = spread * jax.random.normal(stream_key, extent, jnp.float32)
    if shards:
        entries = entries * levels(stream_key, extent, shards, -0.22, 0.18)
    return jnp.clip(strengthened(entries, jax.random.fold_in(stream_key, 3), *heavy), -reach, reach).astype(kind)


def setup_inputs(seed: int = 0) -> dict:
    splits = jax.random.split(jax.random.key(seed), 12)
    tokens = bell_draw_with(splits[0], (TOKENS, D), 1.0, 6.0, ((0, 32), (1, 4)), (0, 1, 32, 2.75))
    cotangent = bell_draw_with(splits[1], (TOKENS, D), 1.0, 6.0, ((0, 32), (1, 4)), (0, 1, 32, 2.75))
    expert_ids_keys = jax.random.split(jax.random.fold_in(splits[2], 1), TOKENS // TOK_DEV)
    expert_ids_turns = jax.random.permutation(jax.random.fold_in(splits[2], 3), TOKENS // TOK_DEV)
    expert_ids = jax.vmap(lambda own, number: assign_block(jax.random.fold_in(splits[2], 2), own, number, TOK_DEV, EXPERTS, TOP_OLD, CAP, 2))(expert_ids_keys, expert_ids_turns).reshape((TOKENS, TOP_OLD))
    gate_weights = jnp.clip(jnp.exp(math.log(1.0) - 2.3025851 * jax.random.uniform(splits[3], (TOKENS, TOP_OLD + 1), jnp.float32) ** levels(splits[3], (TOKENS, TOP_OLD + 1), ((0, 32),), -0.2, 0.2)), 0.1, 1.0)
    shadow_mask = set_ends((jax.random.randint(splits[4], (TOKENS,), 0, 20) < 9).astype(jnp.int32), jax.random.fold_in(splits[4], 1), 0, 1)
    w_gate = noise(splits[5], (EXPERTS, D, FF), D ** -0.5, 0.078125, ((0, 32), (2, 4)))
    w_up = noise(splits[6], (EXPERTS, D, FF), D ** -0.5, 0.078125, ((0, 32), (2, 4)))
    w_down = noise(splits[7], (EXPERTS, FF, D), FF ** -0.5, 0.15625, ((0, 32), (1, 4)))
    s_gate = noise(splits[8], (D, FF), D ** -0.5, 0.078125, ((0, 32), (1, 4)))
    s_up = noise(splits[9], (D, FF), D ** -0.5, 0.078125, ((0, 32), (1, 4)))
    s_down = noise(splits[10], (FF, D), FF ** -0.5, 0.15625, ((0, 4), (1, 32)))
    return dict(tokens=tokens, cotangent=cotangent, expert_ids=expert_ids, gate_weights=gate_weights, shadow_mask=shadow_mask, w_gate=w_gate, w_up=w_up, w_down=w_down, s_gate=s_gate, s_up=s_up, s_down=s_down)


def contract_rows(left, right):
    return lax.dot_general(left, right, (((0,), (0,)), ((), ())), preferred_element_type=jnp.float32)


def swiglu_pass(rows_x, rows_dout, weight_gate, weight_up, weight_down):
    pre_gate = jnp.dot(rows_x, weight_gate, preferred_element_type=jnp.float32)
    pre_up = jnp.dot(rows_x, weight_up, preferred_element_type=jnp.float32)
    sigmoid_gate = jax.nn.sigmoid(pre_gate)
    activated = pre_gate * sigmoid_gate
    hidden = (activated * pre_up).astype(jnp.bfloat16)
    row_count = rows_x.shape[0]
    per_block = weight_down.shape[0] // N_TP
    quarters = jnp.einsum('rqh,qhd->qrd', hidden.astype(jnp.float32).reshape(row_count, N_TP, per_block),
                          weight_down.astype(jnp.float32).reshape(N_TP, per_block, weight_down.shape[1]),
                          precision=lax.Precision.HIGHEST)
    rounded = lax.optimization_barrier(quarters.astype(jnp.bfloat16))
    output = jnp.sum(rounded.astype(jnp.float32), axis=0)
    hidden_grad = lax.dot_general(rows_dout, weight_down, (((1,), (1,)), ((), ())), preferred_element_type=jnp.float32)
    grad_pre_gate = (hidden_grad * pre_up * sigmoid_gate * (1.0 + pre_gate * (1.0 - sigmoid_gate))).astype(jnp.bfloat16)
    grad_pre_up = (hidden_grad * activated).astype(jnp.bfloat16)
    return (output, contract_rows(rows_x, grad_pre_gate), contract_rows(rows_x, grad_pre_up),
            contract_rows(hidden, rows_dout))


def reference(tokens, cotangent, expert_ids, gate_weights, shadow_mask, w_gate, w_up, w_down, s_gate, s_up, s_down):
    picks = expert_ids.reshape(N_EP, TOK_DEV * TOP_OLD)
    onehot = (picks[:, :, None] == jnp.arange(EXPERTS, dtype=jnp.int32)[None, None, :]).astype(jnp.int32)
    slot_rank = jnp.sum((jnp.cumsum(onehot, axis=1) - onehot) * onehot, axis=2)
    position = (jnp.arange(N_EP, dtype=jnp.int32)[:, None] * CAP + slot_rank).reshape(-1).astype(jnp.int32)
    token_of = jnp.repeat(jnp.arange(TOKENS, dtype=jnp.int32), TOP_OLD)
    picks_flat = expert_ids.reshape(-1).astype(jnp.int32)
    row_token = jnp.zeros((EXPERTS, N_EP * CAP), jnp.int32).at[picks_flat, position].set(token_of)
    row_weight = jnp.zeros((EXPERTS, N_EP * CAP), jnp.float32).at[picks_flat, position].set(
        gate_weights[:, :TOP_OLD].reshape(-1))
    row_filled = jnp.zeros((EXPERTS, N_EP * CAP), jnp.float32).at[picks_flat, position].set(1.0)

    def one_expert(item):
        weight_gate, weight_up, weight_down, token_index, weight_row, filled = item
        rows_x = tokens[token_index] * filled[:, None].astype(jnp.bfloat16)
        rows_dout = (weight_row[:, None] * cotangent[token_index].astype(jnp.float32)).astype(jnp.bfloat16)
        output, grad_g, grad_u, grad_d = swiglu_pass(rows_x, rows_dout, weight_gate, weight_up, weight_down)
        return output, grad_g.astype(jnp.bfloat16), grad_u.astype(jnp.bfloat16), grad_d.astype(jnp.bfloat16)

    outputs, grad_gate, grad_up, grad_down = lax.map(
        one_expert, (w_gate, w_up, w_down, row_token, row_weight, row_filled))
    mixed_old = jnp.zeros((TOKENS, D), jnp.float32).at[row_token.reshape(-1)].add(
        (row_weight[:, :, None] * outputs).reshape(-1, D))

    shadow_weight = (gate_weights[:, TOP_OLD] * shadow_mask.astype(jnp.float32)).reshape(N_EP, TOK_DEV)
    blocks_x = tokens.reshape(N_EP, TOK_DEV, D)
    blocks_dy = cotangent.reshape(N_EP, TOK_DEV, D)

    def shadow_block(carry, item):
        block_x, block_dy, block_weight = item
        block_dout = (block_weight[:, None] * block_dy.astype(jnp.float32)).astype(jnp.bfloat16)
        output, grad_g, grad_u, grad_d = swiglu_pass(block_x, block_dout, s_gate, s_up, s_down)
        sums = tuple(total + lax.optimization_barrier(piece.astype(jnp.bfloat16)).astype(jnp.float32)
                     for total, piece in zip(carry, (grad_g, grad_u, grad_d)))
        return sums, block_weight[:, None] * output

    start = (jnp.zeros((D, FF), jnp.float32), jnp.zeros((D, FF), jnp.float32), jnp.zeros((FF, D), jnp.float32))
    shadow_sums, shadow_out = lax.scan(shadow_block, start, (blocks_x, blocks_dy, shadow_weight))
    mixed = (mixed_old + shadow_out.reshape(TOKENS, D)).astype(jnp.bfloat16)
    return (mixed, grad_gate, grad_up, grad_down, shadow_sums[0].astype(jnp.bfloat16),
            shadow_sums[1].astype(jnp.bfloat16), shadow_sums[2].astype(jnp.bfloat16))
```

```python
import jax
import jax.numpy as jnp
from jax import lax
from jax.experimental import pallas as pl
from jax.experimental.pallas import tpu as pltpu
from jax.sharding import PartitionSpec as P

SLOTS = 16
MIX = 13
ROWS = 64
ANY = pl.BlockSpec(memory_space=pl.ANY)
VMEM = pl.BlockSpec(memory_space=pltpu.VMEM)
MESH = pl.DeviceIdType.MESH
BF16, F32 = jnp.bfloat16, jnp.float32


def contract_rows(left, right):
    return lax.dot_general(left, right, (((0,), (0,)), ((), ())), preferred_element_type=F32)


def split_parts(values):
    upper = values.astype(BF16)
    return upper, (values - upper.astype(F32)).astype(BF16)


def ep_peer(ep, k, sign):
    k = (k * MIX) % 32
    z, y, c = ep // 8, (ep // 2) % 4, ep % 2
    dz, dy, dc = k // 8, (k // 2) % 4, k % 2
    return ((z + sign * dz + 4) % 4) * 8 + ((y + sign * dy + 4) % 4) * 2 + (c + dc) % 2


def drain(ref, sem):
    pltpu.make_async_copy(ref, ref, sem).wait()


def dispatch_kernel(tok, cot, rows_x, rows_d, disp, gate, out_x, out_d, full_x, full_d, tok2, cot2, rows2_x, rows2_d,
                    ring_send, ring_recv, own_sem, a_send, a_recv, b_send, b_recv, f_send, f_recv):
    tp, ep = lax.axis_index("tp"), lax.axis_index("ep")
    quarter = tok.shape[1]
    mine = pl.multiple_of(tp * quarter, quarter)
    opposite = pl.multiple_of(((tp + 2) % 4) * quarter, quarter)
    my_rows = pl.multiple_of(ep * SLOTS, SLOTS)

    barrier = pltpu.get_barrier_semaphore()
    for d in (1, 2, 3):
        pl.semaphore_signal(barrier, inc=1, device_id=((tp + d) % 4, ep), device_id_type=MESH)

    def greet(k, carry):
        pl.semaphore_signal(barrier, inc=1, device_id=(tp, ep_peer(ep, k, 1)), device_id_type=MESH)
        return carry

    lax.fori_loop(1, 32, greet, 0)
    pl.semaphore_wait(barrier, 34)

    ring = []
    for d in (2, 1, 3):
        for i, (src, far, full) in enumerate(((tok, tok2, full_x), (cot, cot2, full_d))):
            copy = pltpu.make_async_remote_copy(
                src_ref=src, dst_ref=far if d == 2 else full.at[:, pl.ds(mine, quarter)],
                send_sem=ring_send.at[d - 1, i], recv_sem=ring_recv.at[d - 1, i],
                device_id=((tp + d) % 4, ep), device_id_type=MESH)
            copy.start()
            ring.append((d, copy))

    def send_rows(src_x, src_d, column, send_sem, recv_sem):
        def one(k, carry):
            peer = ep_peer(ep, k, 1)
            theirs = pl.multiple_of(peer * SLOTS, SLOTS)
            for src, out in ((src_x, out_x), (src_d, out_d)):
                pltpu.make_async_remote_copy(
                    src_ref=src.at[pl.ds(theirs, SLOTS), :],
                    dst_ref=out.at[pl.ds(my_rows, SLOTS), pl.ds(column, quarter)],
                    send_sem=send_sem, recv_sem=recv_sem, device_id=(tp, peer), device_id_type=MESH).start()
            return carry
        lax.fori_loop(1, 32, one, 0)

    send_rows(rows_x, rows_d, mine, a_send, a_recv.at[ep])

    local = [
        pltpu.make_async_copy(tok, full_x.at[:, pl.ds(mine, quarter)], own_sem.at[0]),
        pltpu.make_async_copy(cot, full_d.at[:, pl.ds(mine, quarter)], own_sem.at[1]),
        pltpu.make_async_copy(rows_x.at[pl.ds(my_rows, SLOTS), :],
                              out_x.at[pl.ds(my_rows, SLOTS), pl.ds(mine, quarter)], own_sem.at[2]),
        pltpu.make_async_copy(rows_d.at[pl.ds(my_rows, SLOTS), :],
                              out_d.at[pl.ds(my_rows, SLOTS), pl.ds(mine, quarter)], own_sem.at[3]),
    ]
    for copy in local:
        copy.start()

    for d, copy in ring[:2]:
        copy.wait_recv()

    def select(c, carry):
        at = pl.ds(pl.multiple_of(c * 128, 128), 128)
        rows2_x[at, :] = jnp.dot(disp[at, :], tok2[...], preferred_element_type=F32).astype(BF16)
        rows2_d[at, :] = (gate[at, :] * jnp.dot(disp[at, :], cot2[...], preferred_element_type=F32)).astype(BF16)
        return carry

    lax.fori_loop(0, rows2_x.shape[0] // 128, select, 0)
    send_rows(rows2_x, rows2_d, opposite, b_send, b_recv)
    late = [
        pltpu.make_async_copy(tok2, full_x.at[:, pl.ds(opposite, quarter)], own_sem.at[4]),
        pltpu.make_async_copy(cot2, full_d.at[:, pl.ds(opposite, quarter)], own_sem.at[5]),
        pltpu.make_async_copy(rows2_x.at[pl.ds(my_rows, SLOTS), :],
                              out_x.at[pl.ds(my_rows, SLOTS), pl.ds(opposite, quarter)], own_sem.at[6]),
        pltpu.make_async_copy(rows2_d.at[pl.ds(my_rows, SLOTS), :],
                              out_d.at[pl.ds(my_rows, SLOTS), pl.ds(opposite, quarter)], own_sem.at[7]),
    ]
    for copy in late:
        copy.start()
    for copy in local:
        copy.wait()

    def forward(source):
        at = pl.ds(pl.multiple_of(source * SLOTS, SLOTS), SLOTS), pl.ds(mine, quarter)
        for i, d in enumerate((1, 3)):
            for out in (out_x, out_d):
                pltpu.make_async_remote_copy(
                    src_ref=out.at[at], dst_ref=out.at[at], send_sem=f_send.at[i], recv_sem=f_recv.at[i],
                    device_id=((tp + d) % 4, ep), device_id_type=MESH).start()

    forward(ep)

    def relay(k, carry):
        source = ep_peer(ep, k, -1)
        drain(out_x.at[pl.ds(0, SLOTS), pl.ds(0, 2 * quarter)], a_recv.at[source])
        forward(source)
        return carry

    lax.fori_loop(1, 32, relay, 0)

    for copy in late:
        copy.wait()
    for d, copy in ring[:2]:
        copy.wait_send()
    for d, copy in ring[2:]:
        copy.wait()
    others = out_x.at[pl.ds(0, 31 * SLOTS), pl.ds(0, 2 * quarter)]
    everything = out_x.at[:, pl.ds(0, 2 * quarter)]
    drain(others, a_send)
    drain(others, b_send)
    drain(others, b_recv)
    for i in range(2):
        drain(everything, f_send.at[i])
        drain(everything, f_recv.at[i])


def dispatch_rows(tok, cot, rows_x, rows_d, disp, gate):
    count, quarter = tok.shape
    slots = rows_x.shape[0]
    width = 4 * quarter
    dma = pltpu.SemaphoreType.DMA
    return pl.pallas_call(
        dispatch_kernel,
        out_shape=(jax.ShapeDtypeStruct((slots, width), BF16),) * 2 + (jax.ShapeDtypeStruct((count, width), BF16),) * 2,
        in_specs=[VMEM] * 6,
        out_specs=(ANY,) * 4,
        scratch_shapes=[pltpu.VMEM((count, quarter), BF16)] * 2 + [pltpu.VMEM((slots, quarter), BF16)] * 2
        + [dma((3, 2)), dma((3, 2)), dma((8,)), dma, dma((32,)), dma, dma, dma((2,)), dma((2,))],
        compiler_params=pltpu.CompilerParams(collective_id=0, has_side_effects=True),
        name="dispatch_rows",
    )(tok, cot, rows_x, rows_d, disp, gate)


def combine_kernel(routed, shadow, back, shadow_sum, passing, relayed, far, near, total, pass_send, pass_recv, far_send,
                   far_recv, near_send, near_recv, back_send, back_recv, own_sem):
    tp, ep = lax.axis_index("tp"), lax.axis_index("ep")
    quarter = back.shape[1]
    blocks = routed.shape[0] // ROWS
    steps = blocks + shadow.shape[0] // ROWS
    per = ROWS // SLOTS

    barrier = pltpu.get_barrier_semaphore()
    for d in (1, 3):
        pl.semaphore_signal(barrier, inc=1, device_id=((tp + d) % 4, ep), device_id_type=MESH)

    def greet(k, carry):
        pl.semaphore_signal(barrier, inc=1, device_id=(tp, ep_peer(ep, k, 1)), device_id_type=MESH)
        return carry

    lax.fori_loop(1, 32, greet, 0)
    pl.semaphore_wait(barrier, 33)

    def block(i):
        return (i + ep // per) % blocks

    def piece(i, owner):
        columns = pl.ds(pl.multiple_of((owner % 4) * quarter, quarter), quarter)
        if i < blocks:
            return routed.at[pl.ds(pl.multiple_of(block(i) * ROWS, ROWS), ROWS), columns]
        return shadow.at[pl.ds((i - blocks) * ROWS, ROWS), columns]

    def way(i):
        return 1 if i % 2 == 0 else 3

    def send(src, dst, sems, i, d):
        return pltpu.make_async_remote_copy(
            src_ref=src, dst_ref=dst.at[i], send_sem=sems[0].at[i], recv_sem=sems[1].at[i],
            device_id=((tp + d) % 4, ep), device_id_type=MESH)

    passes = [send(piece(i, tp + 2), passing, (pass_send, pass_recv), i, way(i)) for i in range(steps)]
    nears = [send(piece(i, tp + 4 - way(i)), near, (near_send, near_recv), i, 4 - way(i)) for i in range(steps)]
    fars = [send(relayed.at[i], far, (far_send, far_recv), i, way(i)) for i in range(steps)]

    def finish(i):
        fars[i].wait_recv()
        nears[i].wait_recv()
        result = piece(i, tp)[...].astype(F32) + far[i].astype(F32) + near[i].astype(F32)
        if i >= blocks:
            shadow_sum[pl.ds((i - blocks) * ROWS, ROWS), :] = result
            return
        total[i] = result.astype(BF16)
        for j in range(per):
            peer = block(i) * per + j
            source = total.at[i, pl.ds(j * SLOTS, SLOTS), :]
            target = back.at[pl.ds(pl.multiple_of(ep * SLOTS, SLOTS), SLOTS), :]

            @pl.when(peer != ep)
            def _():
                pltpu.make_async_remote_copy(src_ref=source, dst_ref=target, send_sem=back_send, recv_sem=back_recv,
                                             device_id=(tp, peer), device_id_type=MESH).start()

            @pl.when(peer == ep)
            def _():
                pltpu.make_async_copy(source, target, own_sem).start()

    for i in range(steps):
        passes[i].start()
    for i in range(steps):
        nears[i].start()
        passes[i].wait_recv()
        relayed[i] = (piece(i, tp + way(i))[...].astype(F32) + passing[i].astype(F32)).astype(BF16)
        fars[i].start()
        if i >= 2:
            finish(i - 2)
    finish(steps - 2)
    finish(steps - 1)

    for i in range(steps):
        passes[i].wait_send()
        nears[i].wait_send()
        fars[i].wait_send()
    drain(back.at[pl.ds(0, SLOTS), :], own_sem)
    drain(back.at[pl.ds(0, 31 * SLOTS), :], back_send)
    drain(back.at[pl.ds(0, 31 * SLOTS), :], back_recv)


def combine_rows(routed, shadow):
    slots, width = routed.shape
    count, quarter = shadow.shape[0], width // 4
    steps = (slots + count) // ROWS
    dma = pltpu.SemaphoreType.DMA
    return pl.pallas_call(
        combine_kernel,
        out_shape=(jax.ShapeDtypeStruct((slots, quarter), BF16), jax.ShapeDtypeStruct((count, quarter), F32)),
        in_specs=[VMEM] * 2,
        out_specs=(VMEM,) * 2,
        scratch_shapes=[pltpu.VMEM((steps, ROWS, quarter), BF16)] * 4 + [pltpu.VMEM((slots // ROWS, ROWS, quarter), BF16)]
        + [dma((steps,))] * 6 + [dma] * 3,
        compiler_params=pltpu.CompilerParams(collective_id=1, has_side_effects=True),
        name="combine_rows",
    )(routed, shadow)


def outer_kernel(x, d, gate, up, hidden, out):
    part = gate.shape[1]
    out[:, :part] = contract_rows(x[...], gate[...]).astype(BF16)
    out[:, part:2 * part] = contract_rows(x[...], up[...]).astype(BF16)
    out[:, 2 * part:] = contract_rows(d[...], hidden[...]).astype(BF16)


def shadow_grads(x, d, gate, up, hidden):
    count, width = x.shape
    part, tile = gate.shape[1], 640
    wide = pl.BlockSpec((count, tile), lambda i: (0, i))
    whole = pl.BlockSpec((count, part), lambda i: (0, 0))
    return pl.pallas_call(
        outer_kernel, grid=(width // tile,),
        out_shape=jax.ShapeDtypeStruct((width, 3 * part), BF16),
        in_specs=[wide, wide, whole, whole, whole],
        out_specs=pl.BlockSpec((tile, 3 * part), lambda i: (i, 0)),
        cost_estimate=pl.CostEstimate(flops=6 * count * width * part, bytes_accessed=6 * width * part, transcendentals=0),
        name="shadow_grads",
    )(x, d, gate, up, hidden)


def expert_pass(rows_x, rows_dout, weight_gate, weight_up, weight_down):
    pre_gate = jnp.dot(rows_x, weight_gate, preferred_element_type=F32)
    pre_up = jnp.dot(rows_x, weight_up, preferred_element_type=F32)
    sigmoid_gate = jax.nn.sigmoid(pre_gate)
    activated = pre_gate * sigmoid_gate
    hidden = (activated * pre_up).astype(BF16)
    partial_out = jnp.dot(hidden, weight_down, preferred_element_type=F32).astype(BF16)
    hidden_grad = lax.dot_general(rows_dout, weight_down, (((1,), (1,)), ((), ())), preferred_element_type=F32)
    grad_pre_gate = (hidden_grad * pre_up * sigmoid_gate * (1.0 + pre_gate * (1.0 - sigmoid_gate))).astype(BF16)
    grad_pre_up = (hidden_grad * activated).astype(BF16)
    return partial_out, hidden, grad_pre_gate, grad_pre_up


def shards(tokens, cotangent, expert_ids, gate_weights, shadow_mask, w_gate, w_up, w_down, s_gate, s_up, s_down):
    tok_count, top_count = expert_ids.shape
    quarter = tokens.shape[1]
    width = 4 * quarter
    experts = 32
    slot_count = experts * SLOTS
    s_all = lax.all_gather(jnp.concatenate([s_gate, s_up, s_down.T], axis=1), "ep", axis=0, tiled=True)

    picks = expert_ids.reshape(-1)
    onehot = (picks[:, None] == jnp.arange(experts, dtype=jnp.int32)[None, :]).astype(jnp.int32)
    rank = jnp.sum((jnp.cumsum(onehot, axis=0) - onehot) * onehot, axis=1)
    slot_index = (picks * SLOTS + rank).reshape(tok_count, top_count)
    matches = jnp.arange(slot_count, dtype=jnp.int32)[:, None, None] == slot_index[None, :, :]
    dispatch = jnp.any(matches, axis=2).astype(BF16)
    weighting = jnp.sum(jnp.where(matches, gate_weights[None, :, :top_count], 0.0), axis=2)
    slot_gate = jnp.sum(weighting, axis=1, keepdims=True)
    shadow_weight = gate_weights[:, top_count] * shadow_mask.astype(F32)

    rows_x = jnp.dot(dispatch, tokens, preferred_element_type=F32).astype(BF16)
    rows_d = (slot_gate * jnp.dot(dispatch, cotangent, preferred_element_type=F32)).astype(BF16)
    expert_x, expert_d, full_x, full_dy = dispatch_rows(tokens, cotangent, rows_x, rows_d, dispatch, slot_gate)

    partial_out, hidden, grad_pre_gate, grad_pre_up = expert_pass(expert_x, expert_d, w_gate[0], w_up[0], w_down[0])
    grad_gate = contract_rows(expert_x, grad_pre_gate).astype(BF16)[None]
    grad_up = contract_rows(expert_x, grad_pre_up).astype(BF16)[None]
    grad_down = contract_rows(hidden, expert_d).astype(BF16)[None]

    part = s_gate.shape[1]
    shadow_d = (shadow_weight[:, None] * full_dy.astype(F32)).astype(BF16)
    full_gate, full_up, full_down = s_all[:, :part], s_all[:, part:2 * part], s_all[:, 2 * part:].T
    shadow_out, shadow_hidden, shadow_pre_gate, shadow_pre_up = expert_pass(full_x, shadow_d, full_gate, full_up, full_down)
    shadow_sums = lax.psum_scatter(
        shadow_grads(full_x, shadow_d, shadow_pre_gate, shadow_pre_up, shadow_hidden), "ep", scatter_dimension=0, tiled=True)
    grad_s_gate = shadow_sums[:, :part]
    grad_s_up = shadow_sums[:, part:2 * part]
    grad_s_down = shadow_sums[:, 2 * part:].T

    back, shadow_sum = combine_rows(partial_out, shadow_out)
    upper, lower = split_parts(weighting.T)
    combined = jnp.dot(upper, back, preferred_element_type=F32) + jnp.dot(lower, back, preferred_element_type=F32)
    mixed = (combined + shadow_weight[:, None] * shadow_sum).astype(BF16)
    return mixed, grad_gate, grad_up, grad_down, grad_s_gate, grad_s_up, grad_s_down


def solution(mesh):
    return jax.shard_map(
        shards, mesh=mesh,
        in_specs=(P("ep", "tp"), P("ep", "tp"), P("ep", None), P("ep", None), P("ep"), P("ep", None, "tp"),
                  P("ep", None, "tp"), P("ep", "tp", None), P("ep", "tp"), P("ep", "tp"), P("tp", "ep")),
        out_specs=(P("ep", "tp"), P("ep", None, "tp"), P("ep", None, "tp"), P("ep", "tp", None), P("ep", "tp"),
                   P("ep", "tp"), P("tp", "ep")),
        check_vma=False)
```

```python
import jax
import jax.numpy as jnp
from jax import lax
from jax.experimental import pallas as pl
from jax.experimental.pallas import tpu as pltpu
from jax.sharding import PartitionSpec as P

SLOTS = 16
MIX = 13
ROWS = 64
CUTS = (0, 48, 80, 128, 160)
ORDER = sorted(((j, i) for j in range(4) for i in range(4) if j + i > 0), key=lambda ji: (ji[0] + ji[1], -ji[0]))
FIRST_LEG, E_START, W_PER = 6, 1, 1
VMEM_BYTES = 62 * 1024 * 1024
A_LEAD, A_RATE, R_START, R_RATE, R_MID = 4, 2, 5, 1, 20
ANY = pl.BlockSpec(memory_space=pl.ANY)
VMEM = pl.BlockSpec(memory_space=pltpu.VMEM)
MESH = pl.DeviceIdType.MESH
BF16, F32 = jnp.bfloat16, jnp.float32


def contract_rows(left, right):
    return lax.dot_general(left, right, (((0,), (0,)), ((), ())), preferred_element_type=F32)


def split_parts(values):
    upper = values.astype(BF16)
    return upper, (values - upper.astype(F32)).astype(BF16)


def ep_peer(ep, k, sign):
    k = (k * MIX) % 32
    z, y, c = ep // 8, (ep // 2) % 4, ep % 2
    dz, dy, dc = k // 8, (k // 2) % 4, k % 2
    return ((z + sign * dz + 4) % 4) * 8 + ((y + sign * dy + 4) % 4) * 2 + (c + dc) % 2


def drain(ref, sem):
    pltpu.make_async_copy(ref, ref, sem).wait()


def dispatch_kernel(tok, cot, disp, gate, s_gate, s_up, s_down, s_weight, out_x, out_d, out_s, out_g, full_x, full_d,
                    rows_x, rows_d, rows2_x, rows2_d, s_all, acc, hidden, slopes, stage, ring_send, ring_recv, own_sem,
                    a_send, a_recv, b_send, b_recv, f_send, f_recv, w_send, w_recv, pair_send, pair_recv, g_sem):
    tp, ep = lax.axis_index("tp"), lax.axis_index("ep")
    z, y, c = ep // 8, (ep // 2) % 4, ep % 2
    quarter, part, share = tok.shape[1], s_gate.shape[1], s_gate.shape[0]
    mine = pl.multiple_of(tp * quarter, quarter)
    opposite = pl.multiple_of(((tp + 2) % 4) * quarter, quarter)
    my_rows = pl.multiple_of(ep * SLOTS, SLOTS)
    partner = ep + 1 - 2 * c

    barrier = pltpu.get_barrier_semaphore()
    for d in (1, 2, 3):
        pl.semaphore_signal(barrier, inc=1, device_id=((tp + d) % 4, ep), device_id_type=MESH)

    def greet(k, carry):
        pl.semaphore_signal(barrier, inc=1, device_id=(tp, ep_peer(ep, k, 1)), device_id_type=MESH)
        return carry

    lax.fori_loop(1, 32, greet, 0)
    my_share = pl.ds(pl.multiple_of(ep * share, share), share)
    local = [pltpu.make_async_copy(src, s_all.at[my_share, pl.ds(i * part, part)], own_sem.at[i])
             for i, src in enumerate((s_gate, s_up, s_down))]
    local += [pltpu.make_async_copy(tok, full_x.at[:, pl.ds(mine, quarter)], own_sem.at[3]),
              pltpu.make_async_copy(cot, full_d.at[:, pl.ds(mine, quarter)], own_sem.at[4])]
    for copy in local:
        copy.start()
    pl.semaphore_wait(barrier, 34)

    ring = []
    for d in (2, 1, 3):
        for i, (src, full) in enumerate(((tok, full_x), (cot, full_d))):
            copy = pltpu.make_async_remote_copy(
                src_ref=src, dst_ref=full.at[:, pl.ds(mine, quarter)],
                send_sem=ring_send.at[d - 1, i], recv_sem=ring_recv.at[d - 1, i],
                device_id=((tp + d) % 4, ep), device_id_type=MESH)
            copy.start()
            ring.append(copy)

    def colour_step(q, at_first, at_second):
        sign = (1 - 2 * c) * (1 if q % 2 == 0 else -1)
        dz, dy = (at_second, at_first) if q < 2 else (at_first, at_second)
        return ((z + sign * dz + 8) % 4) * 8 + ((y + sign * dy + 8) % 4) * 2 + c

    def pass_on(q, j, i):
        origin = colour_step(q, -j, -i)
        where = s_all.at[pl.ds(pl.multiple_of(origin * share + CUTS[q], 16), CUTS[q + 1] - CUTS[q]), :]
        hops = []
        if i == 0 and j < 3:
            hops.append((colour_step(q, 1, 0), w_send.at[q], w_recv.at[q, (j + 1) * 4]))
        if i < 3:
            hops.append((colour_step(q, 0, 1), w_send.at[q], w_recv.at[q, j * 4 + i + 1]))
        hops.append((partner, pair_send, pair_recv))
        for peer, send_sem, recv_sem in hops:
            pltpu.make_async_remote_copy(src_ref=where, dst_ref=where, send_sem=send_sem, recv_sem=recv_sem,
                                         device_id=(tp, peer), device_id_type=MESH).start()

    for copy in local[:3]:
        copy.wait()
    for q in range(4):
        pass_on(q, 0, 0)

    def select(column, into_x, into_d):
        def one(r, carry):
            at = pl.ds(pl.multiple_of(r * 128, 128), 128)
            cut = pl.ds(column, quarter)
            into_x[at, :] = jnp.dot(disp[at, :], full_x[:, cut], preferred_element_type=F32).astype(BF16)
            into_d[at, :] = (gate[at, :] * jnp.dot(disp[at, :], full_d[:, cut], preferred_element_type=F32)).astype(BF16)
            return carry
        lax.fori_loop(0, into_x.shape[0] // 128, one, 0)

    def send_rows(first, last, src_x, src_d, column, send_sem, recv_sem):
        def one(k, carry):
            peer = ep_peer(ep, k, 1)
            theirs = pl.multiple_of(peer * SLOTS, SLOTS)
            for src, out in ((src_x, out_x), (src_d, out_d)):
                pltpu.make_async_remote_copy(
                    src_ref=src.at[pl.ds(theirs, SLOTS), :],
                    dst_ref=out.at[pl.ds(my_rows, SLOTS), pl.ds(column, quarter)],
                    send_sem=send_sem, recv_sem=recv_sem, device_id=(tp, peer), device_id_type=MESH).start()
            return carry
        lax.fori_loop(first, last, one, 0)

    def keep_rows(src_x, src_d, column, sems):
        copies = [pltpu.make_async_copy(src.at[pl.ds(my_rows, SLOTS), :],
                                        out.at[pl.ds(my_rows, SLOTS), pl.ds(column, quarter)], own_sem.at[sem])
                  for src, out, sem in ((src_x, out_x, sems), (src_d, out_d, sems + 1))]
        for copy in copies:
            copy.start()
        return copies

    def forward(source):
        at = pl.ds(pl.multiple_of(source * SLOTS, SLOTS), SLOTS), pl.ds(mine, quarter)
        for i, d in enumerate((1, 3)):
            for out in (out_x, out_d):
                pltpu.make_async_remote_copy(
                    src_ref=out.at[at], dst_ref=out.at[at], send_sem=f_send.at[i], recv_sem=f_recv.at[i],
                    device_id=((tp + d) % 4, ep), device_id_type=MESH).start()

    def relay(k, carry=0):
        source = ep_peer(ep, k, -1)
        drain(out_x.at[pl.ds(0, SLOTS), pl.ds(0, 2 * quarter)], a_recv.at[source])
        forward(source)
        return carry

    for copy in local[3:]:
        copy.wait()
    select(mine, rows_x, rows_d)
    kept = keep_rows(rows_x, rows_d, mine, 5)
    sent, relayed = 1, 1
    for r, (j, i) in enumerate(ORDER):
        upto = min(32, A_LEAD + A_RATE * (r + 1))
        if upto > sent:
            send_rows(sent, upto, rows_x, rows_d, mine, a_send, a_recv.at[ep])
            sent = upto
        for q in range(4):
            drain(s_all.at[pl.ds(0, CUTS[q + 1] - CUTS[q]), :], w_recv.at[q, j * 4 + i])
            pass_on(q, j, i)
        if r == 0:
            for copy in kept:
                copy.wait()
            forward(ep)
        if r >= R_START:
            lax.fori_loop(relayed, relayed + R_RATE, relay, 0)
            relayed += R_RATE

    for copy in ring[:2]:
        copy.wait_recv()
    select(opposite, rows2_x, rows2_d)
    send_rows(1, 32, rows2_x, rows2_d, opposite, b_send, b_recv)
    kept = keep_rows(rows2_x, rows2_d, opposite, 7)
    for copy in ring[2:]:
        copy.wait_recv()
    lax.fori_loop(relayed, R_MID, relay, 0)
    drain(s_all.at[pl.ds(0, s_all.shape[0] // 2), :], pair_recv)

    tile = 640
    tiles = full_x.shape[1] // tile
    left = (32 - R_MID) // tiles
    acc[...] = jnp.zeros_like(acc)

    def before(t, carry):
        at = pl.ds(pl.multiple_of(t * tile, tile), tile)
        full_d[:, at] = (s_weight[...] * full_d[:, at].astype(F32)).astype(BF16)
        acc[:, :2 * part] += jnp.dot(full_x[:, at], s_all[at, :2 * part], preferred_element_type=F32)
        acc[:, 2 * part:] += jnp.dot(full_d[:, at], s_all[at, 2 * part:], preferred_element_type=F32)
        lax.fori_loop(R_MID + t * left, R_MID + (t + 1) * left, relay, 0)
        return carry

    lax.fori_loop(0, tiles, before, 0)
    lax.fori_loop(R_MID + tiles * left, 32, relay, 0)
    pre_gate, pre_up, grad = acc[:, :part], acc[:, part:2 * part], acc[:, 2 * part:]
    sigmoid = jax.nn.sigmoid(pre_gate)
    active = pre_gate * sigmoid
    hidden[...] = (active * pre_up).astype(BF16)
    slopes[:, :part] = (grad * pre_up * sigmoid * (1.0 + pre_gate * (1.0 - sigmoid))).astype(BF16)
    slopes[:, part:] = (grad * active).astype(BF16)

    def after(t, carry):
        at = pl.ds(pl.multiple_of(t * tile, tile), tile)
        slot = t % 2
        result = pltpu.make_async_copy(stage.at[slot], out_g.at[at, :], g_sem.at[slot])

        @pl.when(t >= 2)
        def _():
            result.wait()

        out_s[:, at] = lax.dot_general(hidden[...], s_all[at, 2 * part:], (((1,), (1,)), ((), ())),
                                       preferred_element_type=F32).astype(BF16)
        stage[slot, :, :2 * part] = contract_rows(full_x[:, at], slopes[...]).astype(BF16)
        stage[slot, :, 2 * part:] = contract_rows(full_d[:, at], hidden[...]).astype(BF16)
        result.start()
        return carry

    lax.fori_loop(0, tiles, after, 0)
    for slot in range(2):
        drain(stage.at[slot], g_sem.at[slot])

    for copy in kept:
        copy.wait()
    for copy in ring:
        copy.wait_send()
    for q in range(4):
        drain(s_all.at[pl.ds(0, 15 * (CUTS[q + 1] - CUTS[q])), :], w_send.at[q])
    drain(s_all.at[pl.ds(0, s_all.shape[0] // 2), :], pair_send)
    others = out_x.at[pl.ds(0, 31 * SLOTS), pl.ds(0, 2 * quarter)]
    everything = out_x.at[:, pl.ds(0, 2 * quarter)]
    drain(others, a_send)
    drain(others, b_send)
    drain(others, b_recv)
    for i in range(2):
        drain(everything, f_send.at[i])
        drain(everything, f_recv.at[i])


def dispatch_rows(tok, cot, disp, gate, s_gate, s_up, s_down, s_weight):
    count, quarter = tok.shape
    slots, part = disp.shape[0], s_gate.shape[1]
    width = 4 * quarter
    dma = pltpu.SemaphoreType.DMA
    vmem = pltpu.VMEM
    return pl.pallas_call(
        dispatch_kernel,
        out_shape=(jax.ShapeDtypeStruct((slots, width), BF16),) * 2
        + (jax.ShapeDtypeStruct((count, width), BF16), jax.ShapeDtypeStruct((width, 3 * part), BF16)),
        in_specs=[VMEM] * 8,
        out_specs=(ANY, ANY, VMEM, ANY),
        scratch_shapes=[vmem((count, width), BF16)] * 2 + [vmem((slots, quarter), BF16)] * 4
        + [vmem((width, 3 * part), BF16), vmem((count, 3 * part), F32), vmem((count, part), BF16),
           vmem((count, 2 * part), BF16), vmem((2, 640, 3 * part), BF16)]
        + [dma((3, 2)), dma((3, 2)), dma((9,)), dma, dma((32,)), dma, dma, dma((2,)), dma((2,)), dma((4,)), dma((4, 16)),
           dma, dma, dma((2,))],
        compiler_params=pltpu.CompilerParams(collective_id=0, has_side_effects=True),
        name="dispatch_rows",
    )(tok, cot, disp, gate, s_gate, s_up, s_down, s_weight)


def combine_kernel(shadow, parts, rows_x, rows_d, w_gate, w_up, w_down, back, shadow_sum, share_out, grad_gate, grad_up,
                   grad_down, routed, all_x, all_d, down, strip_gate, strip_up, acc_gate, acc_up, acc_grad, hidden,
                   slope_gate, slope_up, passing, relayed, far, near, total, held, pair, arrived, put_gate, put_up,
                   put_down, pass_send, pass_recv, far_send, far_recv, near_send, near_recv, back_send,
                   back_recv, own_sem, pair_send, pair_recv, held_sem, s_send, s_recv, load_sem, put_sem):
    tp, ep = lax.axis_index("tp"), lax.axis_index("ep")
    z, y, c = ep // 8, (ep // 2) % 4, ep % 2
    quarter = back.shape[1]
    blocks = routed.shape[0] // ROWS
    steps = blocks + shadow.shape[0] // ROWS
    per = ROWS // SLOTS
    share = share_out.shape[0]
    tile = strip_gate.shape[1]
    tiles = rows_x.shape[1] // tile
    early = steps - blocks

    barrier = pltpu.get_barrier_semaphore()
    for d in (1, 3):
        pl.semaphore_signal(barrier, inc=1, device_id=((tp + d) % 4, ep), device_id_type=MESH)

    def greet(k, carry):
        pl.semaphore_signal(barrier, inc=1, device_id=(tp, ep_peer(ep, k, 1)), device_id_type=MESH)
        return carry

    lax.fori_loop(1, 32, greet, 0)

    def share_rows(chip, core):
        return parts.at[pl.ds(pl.multiple_of((chip * 2 + core) * share, share), share), :]

    def chip_at(k):
        return ((z + k // 4) % 4) * 4 + (y + k % 4) % 4

    def columns_of(t):
        return pl.ds(t * tile, tile)

    def loads(t):
        at, sem = columns_of(t), load_sem.at[t]
        return [pltpu.make_async_copy(src.at[:, at], dst.at[:, at], sem.at[i])
                for i, (src, dst) in enumerate(((rows_x, all_x), (rows_d, all_d), (w_down, down)))]

    def strips(t):
        return [pltpu.make_async_copy(src.at[columns_of(t), :], dst.at[t % 2], load_sem.at[t, 3 + i])
                for i, (src, dst) in enumerate(((w_gate, strip_gate), (w_up, strip_up)))]

    for t in range(tiles):
        for copy in loads(t) + (strips(t) if t < 2 else []):
            copy.start()

    def take(k, carry):
        chip = chip_at(k)
        pltpu.make_async_copy(share_rows(chip, c), held.at[chip], held_sem.at[chip]).start()
        return carry

    lax.fori_loop(0, 16, take, 0)
    pl.semaphore_wait(barrier, 33)

    def swap(k, carry):
        chip = chip_at(k)
        pltpu.make_async_remote_copy(
            src_ref=share_rows(chip, 1 - c), dst_ref=pair.at[chip], send_sem=pair_send, recv_sem=pair_recv.at[chip],
            device_id=(tp, ep + 1 - 2 * c), device_id_type=MESH).start()
        return carry

    lax.fori_loop(0, 16, swap, 0)

    def block(i):
        return (i + ep // per) % blocks

    def piece(i, owner):
        columns = pl.ds(pl.multiple_of((owner % 4) * quarter, quarter), quarter)
        if i >= early:
            return routed.at[pl.ds(pl.multiple_of(block(i) * ROWS, ROWS), ROWS), columns]
        return shadow.at[pl.ds(i * ROWS, ROWS), columns]

    def way(i):
        return 1 if i % 2 == 0 else 3

    def send(src, dst, sems, i, d):
        return pltpu.make_async_remote_copy(
            src_ref=src, dst_ref=dst.at[i], send_sem=sems[0].at[i], recv_sem=sems[1].at[i],
            device_id=((tp + d) % 4, ep), device_id_type=MESH)

    passes = [send(piece(i, tp + 2), passing, (pass_send, pass_recv), i, way(i)) for i in range(steps)]
    nears = [send(piece(i, tp + 4 - way(i)), near, (near_send, near_recv), i, 4 - way(i)) for i in range(steps)]
    fars = [send(relayed.at[i], far, (far_send, far_recv), i, way(i)) for i in range(steps)]

    def finish(i):
        fars[i].wait_recv()
        nears[i].wait_recv()
        result = piece(i, tp)[...].astype(F32) + far[i].astype(F32) + near[i].astype(F32)
        if i < early:
            shadow_sum[pl.ds(i * ROWS, ROWS), :] = result
            return
        total[i - early] = result.astype(BF16)
        for j in range(per):
            peer = block(i) * per + j
            source = total.at[i - early, pl.ds(j * SLOTS, SLOTS), :]
            target = back.at[pl.ds(pl.multiple_of(ep * SLOTS, SLOTS), SLOTS), :]

            @pl.when(peer != ep)
            def _():
                pltpu.make_async_remote_copy(src_ref=source, dst_ref=target, send_sem=back_send, recv_sem=back_recv,
                                             device_id=(tp, peer), device_id_type=MESH).start()

            @pl.when(peer == ep)
            def _():
                pltpu.make_async_copy(source, target, own_sem).start()

    def relay(i):
        passes[i].wait_recv()
        relayed[i] = (piece(i, tp + way(i))[...].astype(F32) + passing[i].astype(F32)).astype(BF16)
        fars[i].start()

    def ahead(t):
        for copy in loads(t) + strips(t):
            copy.wait()
        acc_gate[...] += jnp.dot(all_x[:, columns_of(t)], strip_gate[t % 2], preferred_element_type=F32)
        acc_up[...] += jnp.dot(all_x[:, columns_of(t)], strip_up[t % 2], preferred_element_type=F32)
        acc_grad[...] += lax.dot_general(all_d[:, columns_of(t)], down[:, columns_of(t)], (((1,), (1,)), ((), ())),
                                         preferred_element_type=F32)
        if t + 2 < tiles:
            for copy in strips(t + 2):
                copy.start()

    def activate():
        pre_gate, pre_up, grad = acc_gate[...], acc_up[...], acc_grad[...]
        sigmoid = jax.nn.sigmoid(pre_gate)
        active = pre_gate * sigmoid
        hidden[...] = (active * pre_up).astype(BF16)
        slope_gate[...] = (grad * pre_up * sigmoid * (1.0 + pre_gate * (1.0 - sigmoid))).astype(BF16)
        slope_up[...] = (grad * active).astype(BF16)

    def project(owner):
        at = pl.ds(pl.multiple_of((owner % 4) * quarter, quarter), quarter)
        routed[:, at] = jnp.dot(hidden[...], down[:, at], preferred_element_type=F32).astype(BF16)

    def puts(t):
        slot = t % 2
        return [pltpu.make_async_copy(put_gate.at[slot], grad_gate.at[columns_of(t), :], put_sem.at[slot, 0]),
                pltpu.make_async_copy(put_up.at[slot], grad_up.at[columns_of(t), :], put_sem.at[slot, 1]),
                pltpu.make_async_copy(put_down.at[slot], grad_down.at[:, columns_of(t)], put_sem.at[slot, 2])]

    def weights(t):
        slot = t % 2
        if t >= 2:
            for copy in puts(t - 2):
                copy.wait()
        put_gate[slot] = contract_rows(all_x[:, columns_of(t)], slope_gate[...]).astype(BF16)
        put_up[slot] = contract_rows(all_x[:, columns_of(t)], slope_up[...]).astype(BF16)
        put_down[slot] = contract_rows(hidden[...], all_d[:, columns_of(t)]).astype(BF16)
        for copy in puts(t):
            copy.start()

    def colour_step(q, at_first, at_second):
        sign = (1 - 2 * c) * (1 if q % 2 == 0 else -1)
        dz, dy = (at_second, at_first) if q < 2 else (at_first, at_second)
        return ((z + sign * dz + 8) % 4) * 4 + (y + sign * dy + 8) % 4

    def mine(q, a, b):
        return held.at[colour_step(q, -a, -b), pl.ds(CUTS[q], CUTS[q + 1] - CUTS[q]), :]

    def hand_on(q, a, b, along_first, event):
        peer = colour_step(q, 1, 0) if along_first else colour_step(q, 0, 1)
        pltpu.make_async_remote_copy(
            src_ref=mine(q, a, b), dst_ref=arrived.at[event, pl.ds(CUTS[q], CUTS[q + 1] - CUTS[q]), :],
            send_sem=s_send.at[q], recv_sem=s_recv.at[q, event], device_id=(tp, peer * 2 + c),
            device_id_type=MESH).start()

    def gather(q, a, b, event):
        rows = pl.ds(CUTS[q], CUTS[q + 1] - CUTS[q])
        drain(arrived.at[event, rows, :], s_recv.at[q, event])
        kept = mine(q, a, b)
        kept[...] = (kept[...].astype(F32) + arrived[event, rows, :].astype(F32)).astype(BF16)

    def first_leg(t, b):
        for q in range(4):
            gather(q, (t + 1) % 4, b, (t - 1) * 4 + b)
            if t < 3:
                hand_on(q, t + 1, b, True, t * 4 + b)
            elif b == 1:
                hand_on(q, 0, 1, False, 12)

    def second_leg(t):
        for q in range(4):
            gather(q, 0, (t + 1) % 4, 11 + t)
            if t < 3:
                hand_on(q, 0, t + 1, False, 12 + t)

    def join(k, carry):
        chip = chip_at(k)
        drain(held.at[chip], held_sem.at[chip])
        drain(pair.at[chip], pair_recv.at[chip])
        held[chip] = (held[chip].astype(F32) + pair[chip].astype(F32)).astype(BF16)
        return carry

    for i in range(early):
        passes[i].start()
    for i in range(early):
        nears[i].start()
    for ref in (acc_gate, acc_up, acc_grad):
        ref[...] = jnp.zeros_like(ref)
    plan = [lambda t=t, b=b: first_leg(t, b) for t in (1, 2, 3) for b in (1, 2, 3, 0)]
    plan = plan[:10] + [lambda: second_leg(1), plan[10], lambda: second_leg(2), plan[11], lambda: second_leg(3)]
    for t in range(tiles):
        if 1 <= t <= 4:
            lax.fori_loop(4 * t - 4, 4 * t, join, 0)
        if t == 5:
            for b in (1, 2, 3, 0):
                for q in range(4):
                    hand_on(q, 1, b, True, b)
            for i in range(early):
                relay(i)
        ahead(t)
        if t >= FIRST_LEG and plan:
            plan.pop(0)()
    activate()
    project(tp + 2)
    for i in range(early, steps):
        passes[i].start()
    project(tp + 1)
    project(tp + 3)
    for i in range(early, steps):
        nears[i].start()
    project(tp)
    for i in range(early):
        finish(i)
    todo = [lambda i=i: relay(i) for i in range(early, steps)]
    ends = [lambda i=i: finish(i) for i in range(early, steps)]
    work = [lambda t=t: weights(t) for t in range(tiles)]
    while plan or todo or ends or work:
        for queue, count in ((work, W_PER), (plan, 1), (todo, 1)):
            for one in queue[:count]:
                one()
            del queue[:count]
        if len(plan) < E_START and len(todo) < len(ends):
            ends.pop(0)()
    final = pltpu.make_async_copy(held.at[z * 4 + y], share_out, own_sem)

    for i in range(steps):
        passes[i].wait_send()
        nears[i].wait_send()
        fars[i].wait_send()
    drain(back.at[pl.ds(0, SLOTS), :], own_sem)
    final.start()
    final.wait()
    for copy in puts(tiles - 2) + puts(tiles - 1):
        copy.wait()
    drain(held, pair_send)
    for q in range(4):
        drain(parts.at[pl.ds(0, 15 * (CUTS[q + 1] - CUTS[q])), :], s_send.at[q])
    drain(back.at[pl.ds(0, 31 * SLOTS), :], back_send)
    drain(back.at[pl.ds(0, 31 * SLOTS), :], back_recv)


def combine_rows(shadow, parts, rows_x, rows_d, w_gate, w_up, w_down):
    (slots, width), (count, _) = rows_x.shape, shadow.shape
    quarter, part, share, steps, tile = width // 4, w_gate.shape[1], width // 32, (slots + count) // ROWS, 512
    dma, vmem, like = pltpu.SemaphoreType.DMA, pltpu.VMEM, jax.ShapeDtypeStruct
    return pl.pallas_call(
        combine_kernel,
        out_shape=(like((slots, quarter), BF16), like((count, quarter), F32), like((share, 3 * part), BF16),
                   like((width, part), BF16), like((width, part), BF16), like((part, width), BF16)),
        in_specs=[VMEM] + [ANY] * 6,
        out_specs=(VMEM, VMEM, VMEM, ANY, ANY, ANY),
        scratch_shapes=[vmem((slots, width), BF16)] * 3 + [vmem((part, width), BF16)] + [vmem((2, tile, part), BF16)] * 2
        + [vmem((slots, part), F32)] * 3 + [vmem((slots, part), BF16)] * 3
        + [vmem((steps, ROWS, quarter), BF16)] * 4 + [vmem((slots // ROWS, ROWS, quarter), BF16)]
        + [vmem((16, share, 3 * part), BF16)] * 2 + [vmem((15, share, 3 * part), BF16)]
        + [vmem((2, tile, part), BF16)] * 2 + [vmem((2, part, tile), BF16)]
        + [dma((steps,))] * 6 + [dma] * 3
        + [dma, dma((16,)), dma((16,)), dma((4,)), dma((4, 15)), dma((width // tile, 5)), dma((2, 3))],
        compiler_params=pltpu.CompilerParams(collective_id=1, has_side_effects=True, vmem_limit_bytes=VMEM_BYTES),
        name="combine_rows",
    )(shadow, parts, rows_x, rows_d, w_gate, w_up, w_down)


def shards(tokens, cotangent, expert_ids, gate_weights, shadow_mask, w_gate, w_up, w_down, s_gate, s_up, s_down):
    tok_count, top_count = expert_ids.shape
    quarter = tokens.shape[1]
    width = 4 * quarter
    experts = 32
    slot_count = experts * SLOTS
    picks = expert_ids.reshape(-1)
    onehot = (picks[:, None] == jnp.arange(experts, dtype=jnp.int32)[None, :]).astype(jnp.int32)
    rank = jnp.sum((jnp.cumsum(onehot, axis=0) - onehot) * onehot, axis=1)
    slot_index = (picks * SLOTS + rank).reshape(tok_count, top_count)
    matches = jnp.arange(slot_count, dtype=jnp.int32)[:, None, None] == slot_index[None, :, :]
    dispatch = jnp.any(matches, axis=2).astype(BF16)
    weighting = jnp.sum(jnp.where(matches, gate_weights[None, :, :top_count], 0.0), axis=2)
    slot_gate = jnp.sum(weighting, axis=1, keepdims=True)
    shadow_weight = gate_weights[:, top_count] * shadow_mask.astype(F32)

    expert_x, expert_d, shadow_out, shadow_part = dispatch_rows(
        tokens, cotangent, dispatch, slot_gate, s_gate, s_up, s_down.T, shadow_weight[:, None])
    part = s_gate.shape[1]

    back, shadow_sum, shadow_sums, grad_gate, grad_up, grad_down = combine_rows(
        shadow_out, shadow_part, expert_x, expert_d, w_gate[0], w_up[0], w_down[0])
    grad_gate, grad_up, grad_down = grad_gate[None], grad_up[None], grad_down[None]
    grad_s_gate = shadow_sums[:, :part]
    grad_s_up = shadow_sums[:, part:2 * part]
    grad_s_down = shadow_sums[:, 2 * part:].T

    upper, lower = split_parts(weighting.T)
    combined = jnp.dot(upper, back, preferred_element_type=F32) + jnp.dot(lower, back, preferred_element_type=F32)
    mixed = (combined + shadow_weight[:, None] * shadow_sum).astype(BF16)
    return mixed, grad_gate, grad_up, grad_down, grad_s_gate, grad_s_up, grad_s_down


def solution(mesh):
    return jax.shard_map(
        shards, mesh=mesh,
        in_specs=(P("ep", "tp"), P("ep", "tp"), P("ep", None), P("ep", None), P("ep"), P("ep", None, "tp"),
                  P("ep", None, "tp"), P("ep", "tp", None), P("ep", "tp"), P("ep", "tp"), P("tp", "ep")),
        out_specs=(P("ep", "tp"), P("ep", None, "tp"), P("ep", None, "tp"), P("ep", "tp", None), P("ep", "tp"),
                   P("ep", "tp"), P("tp", "ep")),
        check_vma=False)
```

```python
import jax
import jax.numpy as jnp
from jax import lax
from jax.experimental import pallas as pl
from jax.experimental.pallas import tpu as pltpu
from jax.sharding import PartitionSpec as P

SLOTS = 16
MIX = 13
ROWS = 64
CUTS = (0, 48, 80, 128, 160)
ORDER = sorted(((j, i) for j in range(4) for i in range(4) if j + i > 0), key=lambda ji: (ji[0] + ji[1], -ji[0]))
FIRST_LEG, E_START, W_PER = 10, 4, 1
VMEM_BYTES = 62 * 1024 * 1024
A_LEAD, A_RATE, R_START, R_RATE, R_MID = 16, 4, 2, 2, 28
B_AT = 14
ANY = pl.BlockSpec(memory_space=pl.ANY)
VMEM = pl.BlockSpec(memory_space=pltpu.VMEM)
MESH = pl.DeviceIdType.MESH
BF16, F32 = jnp.bfloat16, jnp.float32


def contract_rows(left, right):
    return lax.dot_general(left, right, (((0,), (0,)), ((), ())), preferred_element_type=F32)


def split_parts(values):
    upper = values.astype(BF16)
    return upper, (values - upper.astype(F32)).astype(BF16)


def ep_peer(ep, k, sign):
    k = (k * MIX) % 32
    z, y, c = ep // 8, (ep // 2) % 4, ep % 2
    dz, dy, dc = k // 8, (k // 2) % 4, k % 2
    return ((z + sign * dz + 4) % 4) * 8 + ((y + sign * dy + 4) % 4) * 2 + (c + dc) % 2


def drain(ref, sem):
    pltpu.make_async_copy(ref, ref, sem).wait()


def route(ids, gates, mask, disp, gate, s_weight, upper, lower):
    count, slots = disp.shape[1], disp.shape[0]
    experts = slots // SLOTS
    expert = lax.broadcasted_iota(jnp.int32, (experts, count), 0)
    picked = jnp.zeros((experts, count), F32)
    given = jnp.zeros((experts, count), F32)
    for j in range(ids.shape[0]):
        hit = expert == ids[j:j + 1, :]
        picked = picked + jnp.where(hit, 1.0, 0.0)
        given = given + jnp.where(hit, gates[j:j + 1, :], 0.0)
    first = lax.broadcasted_iota(jnp.int32, (count, count), 0)
    second = lax.broadcasted_iota(jnp.int32, (count, count), 1)
    earlier = jnp.where(first < second, 1.0, 0.0).astype(BF16)
    rank = jnp.dot(picked.astype(BF16), earlier, preferred_element_type=F32)
    slot = lax.broadcasted_iota(jnp.int32, (slots, experts), 0)
    owner = lax.broadcasted_iota(jnp.int32, (slots, experts), 1)
    spread = jnp.where(slot // SLOTS == owner, 1.0, 0.0).astype(BF16)

    def widen(values):
        return jnp.dot(spread, values.astype(BF16), preferred_element_type=F32)

    place = (lax.broadcasted_iota(jnp.int32, (slots, count), 0) % SLOTS).astype(F32)
    filled = jnp.where((widen(picked) > 0.5) & (widen(rank) == place), 1.0, 0.0)
    top, rest = split_parts(given)
    middle, last = split_parts(given - top.astype(F32) - rest.astype(F32))
    weight = filled * ((widen(top) + widen(rest)) + widen(middle))
    disp[...] = filled.astype(BF16)
    gate[...] = jnp.sum(weight, axis=1, keepdims=True)
    upper[...], lower[...] = split_parts(weight)
    shadow = gates[ids.shape[0]:ids.shape[0] + 1, :] * mask[...].astype(F32)
    s_weight[...] = jnp.sum(jnp.where(first == second, shadow, 0.0), axis=1, keepdims=True)


def dispatch_kernel(tok, cot, ids, gates, mask, s_gate, s_up, s_down, out_x, out_d, out_s, out_g, upper, lower, s_weight,
                    disp, gate, full_x, full_d, rows_x, rows_d, rows2_x, rows2_d, s_all, acc, hidden, slopes, stage, ring_send, ring_recv, own_sem,
                    a_send, a_recv, b_send, b_recv, f_send, f_recv, w_send, w_recv, pair_send, pair_recv, g_sem):
    tp, ep = lax.axis_index("tp"), lax.axis_index("ep")
    z, y, c = ep // 8, (ep // 2) % 4, ep % 2
    quarter, part, share = tok.shape[1], s_gate.shape[1], s_gate.shape[0]
    mine = pl.multiple_of(tp * quarter, quarter)
    opposite = pl.multiple_of(((tp + 2) % 4) * quarter, quarter)
    my_rows = pl.multiple_of(ep * SLOTS, SLOTS)
    partner = ep + 1 - 2 * c

    barrier = pltpu.get_barrier_semaphore()
    for d in (1, 2, 3):
        pl.semaphore_signal(barrier, inc=1, device_id=((tp + d) % 4, ep), device_id_type=MESH)

    def greet(k, carry):
        pl.semaphore_signal(barrier, inc=1, device_id=(tp, ep_peer(ep, k, 1)), device_id_type=MESH)
        return carry

    lax.fori_loop(1, 32, greet, 0)
    my_share = pl.ds(pl.multiple_of(ep * share, share), share)
    local = [pltpu.make_async_copy(src, s_all.at[my_share, pl.ds(i * part, part)], own_sem.at[i])
             for i, src in enumerate((s_gate, s_up, s_down))]
    local += [pltpu.make_async_copy(tok, full_x.at[:, pl.ds(mine, quarter)], own_sem.at[3]),
              pltpu.make_async_copy(cot, full_d.at[:, pl.ds(mine, quarter)], own_sem.at[4])]
    for copy in local:
        copy.start()
    pl.semaphore_wait(barrier, 34)

    ring = []
    for d in (2, 1, 3):
        for i, (src, full) in enumerate(((tok, full_x), (cot, full_d))):
            copy = pltpu.make_async_remote_copy(
                src_ref=src, dst_ref=full.at[:, pl.ds(mine, quarter)],
                send_sem=ring_send.at[d - 1, i], recv_sem=ring_recv.at[d - 1, i],
                device_id=((tp + d) % 4, ep), device_id_type=MESH)
            copy.start()
            ring.append(copy)

    def colour_step(q, at_first, at_second):
        sign = (1 - 2 * c) * (1 if q % 2 == 0 else -1)
        dz, dy = (at_second, at_first) if q < 2 else (at_first, at_second)
        return ((z + sign * dz + 8) % 4) * 8 + ((y + sign * dy + 8) % 4) * 2 + c

    def pass_on(q, j, i):
        origin = colour_step(q, -j, -i)
        where = s_all.at[pl.ds(pl.multiple_of(origin * share + CUTS[q], 16), CUTS[q + 1] - CUTS[q]), :]
        hops = []
        if i == 0 and j < 3:
            hops.append((colour_step(q, 1, 0), w_send.at[q], w_recv.at[q, (j + 1) * 4]))
        if i < 3:
            hops.append((colour_step(q, 0, 1), w_send.at[q], w_recv.at[q, j * 4 + i + 1]))
        hops.append((partner, pair_send, pair_recv))
        for peer, send_sem, recv_sem in hops:
            pltpu.make_async_remote_copy(src_ref=where, dst_ref=where, send_sem=send_sem, recv_sem=recv_sem,
                                         device_id=(tp, peer), device_id_type=MESH).start()

    for copy in local[:3]:
        copy.wait()
    for q in range(4):
        pass_on(q, 0, 0)

    def select(column, into_x, into_d):
        def one(r, carry):
            at = pl.ds(pl.multiple_of(r * 128, 128), 128)
            cut = pl.ds(column, quarter)
            into_x[at, :] = jnp.dot(disp[at, :], full_x[:, cut], preferred_element_type=F32).astype(BF16)
            into_d[at, :] = (gate[at, :] * jnp.dot(disp[at, :], full_d[:, cut], preferred_element_type=F32)).astype(BF16)
            return carry
        lax.fori_loop(0, into_x.shape[0] // 128, one, 0)

    def send_rows(first, last, src_x, src_d, column, send_sem, recv_sem):
        def one(k, carry):
            peer = ep_peer(ep, k, 1)
            theirs = pl.multiple_of(peer * SLOTS, SLOTS)
            for src, out in ((src_x, out_x), (src_d, out_d)):
                pltpu.make_async_remote_copy(
                    src_ref=src.at[pl.ds(theirs, SLOTS), :],
                    dst_ref=out.at[pl.ds(my_rows, SLOTS), pl.ds(column, quarter)],
                    send_sem=send_sem, recv_sem=recv_sem, device_id=(tp, peer), device_id_type=MESH).start()
            return carry
        lax.fori_loop(first, last, one, 0)

    def keep_rows(src_x, src_d, column, sems):
        copies = [pltpu.make_async_copy(src.at[pl.ds(my_rows, SLOTS), :],
                                        out.at[pl.ds(my_rows, SLOTS), pl.ds(column, quarter)], own_sem.at[sem])
                  for src, out, sem in ((src_x, out_x, sems), (src_d, out_d, sems + 1))]
        for copy in copies:
            copy.start()
        return copies

    def forward(source):
        at = pl.ds(pl.multiple_of(source * SLOTS, SLOTS), SLOTS), pl.ds(mine, quarter)
        for i, d in enumerate((1, 3)):
            for out in (out_x, out_d):
                pltpu.make_async_remote_copy(
                    src_ref=out.at[at], dst_ref=out.at[at], send_sem=f_send.at[i], recv_sem=f_recv.at[i],
                    device_id=((tp + d) % 4, ep), device_id_type=MESH).start()

    def relay(k, carry=0):
        source = ep_peer(ep, k, -1)
        drain(out_x.at[pl.ds(0, SLOTS), pl.ds(0, 2 * quarter)], a_recv.at[source])
        forward(source)
        return carry

    route(ids, gates, mask, disp, gate, s_weight, upper, lower)
    for copy in local[3:]:
        copy.wait()
    select(mine, rows_x, rows_d)
    kept = keep_rows(rows_x, rows_d, mine, 5)
    sent, relayed = 1, 1
    for r, (j, i) in enumerate(ORDER):
        upto = min(32, A_LEAD + A_RATE * (r + 1))
        if upto > sent:
            send_rows(sent, upto, rows_x, rows_d, mine, a_send, a_recv.at[ep])
            sent = upto
        for q in range(4):
            drain(s_all.at[pl.ds(0, CUTS[q + 1] - CUTS[q]), :], w_recv.at[q, j * 4 + i])
            pass_on(q, j, i)
        if r == 0:
            for copy in kept:
                copy.wait()
            forward(ep)
        if r == B_AT:
            for copy in ring[:2]:
                copy.wait_recv()
            select(opposite, rows2_x, rows2_d)
            send_rows(1, 32, rows2_x, rows2_d, opposite, b_send, b_recv)
            kept = keep_rows(rows2_x, rows2_d, opposite, 7)
        if r >= R_START:
            lax.fori_loop(relayed, relayed + R_RATE, relay, 0)
            relayed += R_RATE

    for copy in ring[2:]:
        copy.wait_recv()
    lax.fori_loop(relayed, R_MID, relay, 0)
    drain(s_all.at[pl.ds(0, s_all.shape[0] // 2), :], pair_recv)

    tile = 640
    tiles = full_x.shape[1] // tile
    left = (32 - R_MID) // tiles
    acc[...] = jnp.zeros_like(acc)

    def before(t, carry):
        at = pl.ds(pl.multiple_of(t * tile, tile), tile)
        full_d[:, at] = (s_weight[...] * full_d[:, at].astype(F32)).astype(BF16)
        acc[:, :2 * part] += jnp.dot(full_x[:, at], s_all[at, :2 * part], preferred_element_type=F32)
        acc[:, 2 * part:] += jnp.dot(full_d[:, at], s_all[at, 2 * part:], preferred_element_type=F32)
        lax.fori_loop(R_MID + t * left, R_MID + (t + 1) * left, relay, 0)
        return carry

    lax.fori_loop(0, tiles, before, 0)
    lax.fori_loop(R_MID + tiles * left, 32, relay, 0)
    pre_gate, pre_up, grad = acc[:, :part], acc[:, part:2 * part], acc[:, 2 * part:]
    sigmoid = jax.nn.sigmoid(pre_gate)
    active = pre_gate * sigmoid
    hidden[...] = (active * pre_up).astype(BF16)
    slopes[:, :part] = (grad * pre_up * sigmoid * (1.0 + pre_gate * (1.0 - sigmoid))).astype(BF16)
    slopes[:, part:] = (grad * active).astype(BF16)

    def after(t, carry):
        at = pl.ds(pl.multiple_of(t * tile, tile), tile)
        slot = t % 2
        result = pltpu.make_async_copy(stage.at[slot], out_g.at[at, :], g_sem.at[slot])

        @pl.when(t >= 2)
        def _():
            result.wait()

        out_s[:, at] = lax.dot_general(hidden[...], s_all[at, 2 * part:], (((1,), (1,)), ((), ())),
                                       preferred_element_type=F32).astype(BF16)
        stage[slot, :, :2 * part] = contract_rows(full_x[:, at], slopes[...]).astype(BF16)
        stage[slot, :, 2 * part:] = contract_rows(full_d[:, at], hidden[...]).astype(BF16)
        result.start()
        return carry

    lax.fori_loop(0, tiles, after, 0)
    for slot in range(2):
        drain(stage.at[slot], g_sem.at[slot])

    for copy in kept:
        copy.wait()
    for copy in ring:
        copy.wait_send()
    for q in range(4):
        drain(s_all.at[pl.ds(0, 15 * (CUTS[q + 1] - CUTS[q])), :], w_send.at[q])
    drain(s_all.at[pl.ds(0, s_all.shape[0] // 2), :], pair_send)
    others = out_x.at[pl.ds(0, 31 * SLOTS), pl.ds(0, 2 * quarter)]
    everything = out_x.at[:, pl.ds(0, 2 * quarter)]
    drain(others, a_send)
    drain(others, b_send)
    drain(others, b_recv)
    for i in range(2):
        drain(everything, f_send.at[i])
        drain(everything, f_recv.at[i])


def dispatch_rows(tok, cot, ids, gates, mask, s_gate, s_up, s_down):
    count, quarter = tok.shape
    slots, part = 32 * SLOTS, s_gate.shape[1]
    width = 4 * quarter
    dma = pltpu.SemaphoreType.DMA
    vmem = pltpu.VMEM
    return pl.pallas_call(
        dispatch_kernel,
        out_shape=(jax.ShapeDtypeStruct((slots, width), BF16),) * 2
        + (jax.ShapeDtypeStruct((count, width), BF16), jax.ShapeDtypeStruct((width, 3 * part), BF16))
        + (jax.ShapeDtypeStruct((slots, count), BF16),) * 2 + (jax.ShapeDtypeStruct((count, 1), F32),),
        in_specs=[VMEM] * 8,
        out_specs=(ANY, ANY, VMEM, ANY, VMEM, VMEM, VMEM),
        scratch_shapes=[vmem((slots, count), BF16), vmem((slots, 1), F32)] + [vmem((count, width), BF16)] * 2 + [vmem((slots, quarter), BF16)] * 4
        + [vmem((width, 3 * part), BF16), vmem((count, 3 * part), F32), vmem((count, part), BF16),
           vmem((count, 2 * part), BF16), vmem((2, 640, 3 * part), BF16)]
        + [dma((3, 2)), dma((3, 2)), dma((9,)), dma, dma((32,)), dma, dma, dma((2,)), dma((2,)), dma((4,)), dma((4, 16)),
           dma, dma, dma((2,))],
        compiler_params=pltpu.CompilerParams(collective_id=0, has_side_effects=True),
        name="dispatch_rows",
    )(tok, cot, ids, gates, mask, s_gate, s_up, s_down)


def combine_kernel(shadow, upper, lower, s_weight, parts, rows_x, rows_d, w_gate, w_up, w_down, mixed, share_out,
                   grad_gate, grad_up, grad_down, back, shadow_sum, routed, all_x, all_d, down, strip, acc, acc_grad,
                   hidden, slopes, passing, relayed, far, near, total, held, pair, arrived, put_gate, put_up,
                   put_down, pass_send, pass_recv, far_send, far_recv, near_send, near_recv, back_send,
                   back_recv, own_sem, pair_send, pair_recv, held_sem, s_send, s_recv, load_sem, put_sem):
    tp, ep = lax.axis_index("tp"), lax.axis_index("ep")
    z, y, c = ep // 8, (ep // 2) % 4, ep % 2
    quarter = back.shape[1]
    blocks = routed.shape[0] // ROWS
    steps = blocks + shadow.shape[0] // ROWS
    per = ROWS // SLOTS
    share = share_out.shape[0]
    tile, part = strip.shape[1], hidden.shape[1]
    tiles = rows_x.shape[1] // tile
    early = steps - blocks

    barrier = pltpu.get_barrier_semaphore()
    for d in (1, 3):
        pl.semaphore_signal(barrier, inc=1, device_id=((tp + d) % 4, ep), device_id_type=MESH)

    def greet(k, carry):
        pl.semaphore_signal(barrier, inc=1, device_id=(tp, ep_peer(ep, k, 1)), device_id_type=MESH)
        return carry

    lax.fori_loop(1, 32, greet, 0)

    def share_rows(chip, core):
        return parts.at[pl.ds(pl.multiple_of((chip * 2 + core) * share, share), share), :]

    def chip_at(k):
        return ((z + k // 4) % 4) * 4 + (y + k % 4) % 4

    def columns_of(t):
        return pl.ds(t * tile, tile)

    def loads(t):
        at, sem = columns_of(t), load_sem.at[t]
        return [pltpu.make_async_copy(src.at[:, at], dst.at[:, at], sem.at[i])
                for i, (src, dst) in enumerate(((rows_x, all_x), (rows_d, all_d), (w_down, down)))]

    def strips(t):
        return [pltpu.make_async_copy(src.at[columns_of(t), :], strip.at[t % 2, :, pl.ds(i * part, part)],
                                      load_sem.at[t, 3 + i]) for i, src in enumerate((w_gate, w_up))]

    for t in range(tiles):
        for copy in (loads(t) if t < 3 else []) + (strips(t) if t < 2 else []):
            copy.start()

    def take(k, carry):
        chip = chip_at(k)
        pltpu.make_async_copy(share_rows(chip, c), held.at[chip], held_sem.at[chip]).start()
        return carry

    lax.fori_loop(0, 16, take, 0)
    pl.semaphore_wait(barrier, 33)

    def swap(k, carry):
        chip = chip_at(k)
        pltpu.make_async_remote_copy(
            src_ref=share_rows(chip, 1 - c), dst_ref=pair.at[chip], send_sem=pair_send, recv_sem=pair_recv.at[chip],
            device_id=(tp, ep + 1 - 2 * c), device_id_type=MESH).start()
        return carry

    lax.fori_loop(0, 16, swap, 0)

    def block(i):
        return (i + ep // per) % blocks

    def piece(i, owner):
        columns = pl.ds(pl.multiple_of((owner % 4) * quarter, quarter), quarter)
        if i >= early:
            return routed.at[pl.ds(pl.multiple_of(block(i) * ROWS, ROWS), ROWS), columns]
        return shadow.at[pl.ds(i * ROWS, ROWS), columns]

    def way(i):
        return 1 if i % 2 == 0 else 3

    def send(src, dst, sems, i, d):
        return pltpu.make_async_remote_copy(
            src_ref=src, dst_ref=dst.at[i], send_sem=sems[0].at[i], recv_sem=sems[1].at[i],
            device_id=((tp + d) % 4, ep), device_id_type=MESH)

    passes = [send(piece(i, tp + 2), passing, (pass_send, pass_recv), i, way(i)) for i in range(steps)]
    nears = [send(piece(i, tp + 4 - way(i)), near, (near_send, near_recv), i, 4 - way(i)) for i in range(steps)]
    fars = [send(relayed.at[i], far, (far_send, far_recv), i, way(i)) for i in range(steps)]

    def finish(i):
        fars[i].wait_recv()
        nears[i].wait_recv()
        result = piece(i, tp)[...].astype(F32) + far[i].astype(F32) + near[i].astype(F32)
        if i < early:
            shadow_sum[pl.ds(i * ROWS, ROWS), :] = result
            return
        total[i - early] = result.astype(BF16)
        for j in range(per):
            peer = block(i) * per + j
            source = total.at[i - early, pl.ds(j * SLOTS, SLOTS), :]
            target = back.at[pl.ds(pl.multiple_of(ep * SLOTS, SLOTS), SLOTS), :]

            @pl.when(peer != ep)
            def _():
                pltpu.make_async_remote_copy(src_ref=source, dst_ref=target, send_sem=back_send, recv_sem=back_recv,
                                             device_id=(tp, peer), device_id_type=MESH).start()

            @pl.when(peer == ep)
            def _():
                pltpu.make_async_copy(source, target, own_sem).start()

    def relay(i):
        passes[i].wait_recv()
        relayed[i] = (piece(i, tp + way(i))[...].astype(F32) + passing[i].astype(F32)).astype(BF16)
        fars[i].start()
        if i >= early:
            nears[i].start()

    def ahead(t):
        for copy in loads(t) + strips(t):
            copy.wait()
        acc[...] += jnp.dot(all_x[:, columns_of(t)], strip[t % 2], preferred_element_type=F32)
        acc_grad[...] += lax.dot_general(all_d[:, columns_of(t)], down[:, columns_of(t)], (((1,), (1,)), ((), ())),
                                         preferred_element_type=F32)
        if t + 2 < tiles:
            for copy in strips(t + 2):
                copy.start()
        if t + 3 < tiles:
            for copy in loads(t + 3):
                copy.start()

    def activate():
        pre_gate, pre_up, grad = acc[:, :part], acc[:, part:], acc_grad[...]
        sigmoid = jax.nn.sigmoid(pre_gate)
        active = pre_gate * sigmoid
        hidden[...] = (active * pre_up).astype(BF16)
        slopes[:, :part] = (grad * pre_up * sigmoid * (1.0 + pre_gate * (1.0 - sigmoid))).astype(BF16)
        slopes[:, part:] = (grad * active).astype(BF16)

    def project(owner):
        at = pl.ds(pl.multiple_of((owner % 4) * quarter, quarter), quarter)
        routed[:, at] = jnp.dot(hidden[...], down[:, at], preferred_element_type=F32).astype(BF16)

    def puts(t):
        slot = t % 2
        return [pltpu.make_async_copy(put_gate.at[slot], grad_gate.at[columns_of(t), :], put_sem.at[slot, 0]),
                pltpu.make_async_copy(put_up.at[slot], grad_up.at[columns_of(t), :], put_sem.at[slot, 1]),
                pltpu.make_async_copy(put_down.at[slot], grad_down.at[:, columns_of(t)], put_sem.at[slot, 2])]

    def weights(t):
        slot = t % 2
        if t >= 2:
            for copy in puts(t - 2):
                copy.wait()
        both = contract_rows(all_x[:, columns_of(t)], slopes[...]).astype(BF16)
        put_gate[slot], put_up[slot] = both[:, :part], both[:, part:]
        put_down[slot] = contract_rows(hidden[...], all_d[:, columns_of(t)]).astype(BF16)
        for copy in puts(t):
            copy.start()

    def colour_step(q, at_first, at_second):
        sign = (1 - 2 * c) * (1 if q % 2 == 0 else -1)
        dz, dy = (at_second, at_first) if q < 2 else (at_first, at_second)
        return ((z + sign * dz + 8) % 4) * 4 + (y + sign * dy + 8) % 4

    def mine(q, a, b):
        return held.at[colour_step(q, -a, -b), pl.ds(CUTS[q], CUTS[q + 1] - CUTS[q]), :]

    def hand_on(q, a, b, along_first, event):
        peer = colour_step(q, 1, 0) if along_first else colour_step(q, 0, 1)
        pltpu.make_async_remote_copy(
            src_ref=mine(q, a, b), dst_ref=arrived.at[event, pl.ds(CUTS[q], CUTS[q + 1] - CUTS[q]), :],
            send_sem=s_send.at[q], recv_sem=s_recv.at[q, event], device_id=(tp, peer * 2 + c),
            device_id_type=MESH).start()

    def gather(q, a, b, event):
        rows = pl.ds(CUTS[q], CUTS[q + 1] - CUTS[q])
        drain(arrived.at[event, rows, :], s_recv.at[q, event])
        kept = mine(q, a, b)
        kept[...] = (kept[...].astype(F32) + arrived[event, rows, :].astype(F32)).astype(BF16)

    def first_leg(t, b):
        for q in range(4):
            gather(q, (t + 1) % 4, b, (t - 1) * 4 + b)
            if t < 3:
                hand_on(q, t + 1, b, True, t * 4 + b)
            elif b == 1:
                hand_on(q, 0, 1, False, 12)

    def second_leg(t):
        for q in range(4):
            gather(q, 0, (t + 1) % 4, 11 + t)
            if t < 3:
                hand_on(q, 0, t + 1, False, 12 + t)

    def join(k, carry):
        chip = chip_at(k)
        drain(held.at[chip], held_sem.at[chip])
        drain(pair.at[chip], pair_recv.at[chip])
        held[chip] = (held[chip].astype(F32) + pair[chip].astype(F32)).astype(BF16)
        return carry

    for i in range(early):
        passes[i].start()
    for i in range(early):
        nears[i].start()
    for ref in (acc, acc_grad):
        ref[...] = jnp.zeros_like(ref)
    plan = [lambda t=t, b=b: first_leg(t, b) for t in (1, 2, 3) for b in (1, 2, 3, 0)]
    plan = plan[:10] + [lambda: second_leg(1), plan[10], lambda: second_leg(2), plan[11], lambda: second_leg(3)]
    for t in range(tiles):
        if t >= 2:
            lax.fori_loop(2 * t - 4, 2 * t - 2, join, 0)
        if t == tiles - 1:
            for b in (1, 2, 3, 0):
                for q in range(4):
                    hand_on(q, 1, b, True, b)
            for i in range(early):
                relay(i)
        ahead(t)
        if t >= FIRST_LEG and plan:
            plan.pop(0)()
    activate()
    project(tp + 2)
    for i in range(early, steps):
        passes[i].start()
    project(tp + 1)
    project(tp + 3)
    project(tp)
    for i in range(early):
        finish(i)
    todo = [lambda i=i: relay(i) for i in range(early, steps)]
    ends = [lambda i=i: finish(i) for i in range(early, steps)]
    work = [lambda t=t: weights(t) for t in range(tiles)]
    while plan or todo or ends or work:
        for queue, count in ((work, W_PER), (plan, 1), (todo, 1)):
            for one in queue[:count]:
                one()
            del queue[:count]
        if len(plan) < E_START and len(todo) < len(ends):
            ends.pop(0)()
    final = pltpu.make_async_copy(held.at[z * 4 + y], share_out, own_sem)

    for i in range(steps):
        passes[i].wait_send()
        nears[i].wait_send()
        fars[i].wait_send()
    drain(back.at[pl.ds(0, SLOTS), :], own_sem)
    final.start()
    final.wait()
    for copy in puts(tiles - 2) + puts(tiles - 1):
        copy.wait()
    drain(held, pair_send)
    for q in range(4):
        drain(parts.at[pl.ds(0, 15 * (CUTS[q + 1] - CUTS[q])), :], s_send.at[q])
    drain(back.at[pl.ds(0, 31 * SLOTS), :], back_send)
    drain(back.at[pl.ds(0, 31 * SLOTS), :], back_recv)
    result = contract_rows(upper[...], back[...]) + contract_rows(lower[...], back[...])
    mixed[...] = (result + s_weight[...] * shadow_sum[...]).astype(BF16)


def combine_rows(shadow, upper, lower, s_weight, parts, rows_x, rows_d, w_gate, w_up, w_down):
    (slots, width), (count, _) = rows_x.shape, shadow.shape
    quarter, part, share, steps, tile = width // 4, w_gate.shape[1], width // 32, (slots + count) // ROWS, 512
    dma, vmem, like = pltpu.SemaphoreType.DMA, pltpu.VMEM, jax.ShapeDtypeStruct
    return pl.pallas_call(
        combine_kernel,
        out_shape=(like((count, quarter), BF16), like((share, 3 * part), BF16),
                   like((width, part), BF16), like((width, part), BF16), like((part, width), BF16)),
        in_specs=[VMEM] * 4 + [ANY] * 6,
        out_specs=(VMEM, VMEM, ANY, ANY, ANY),
        scratch_shapes=[vmem((slots, quarter), BF16), vmem((count, quarter), F32)]
        + [vmem((slots, width), BF16)] * 3 + [vmem((part, width), BF16), vmem((2, tile, 2 * part), BF16)]
        + [vmem((slots, 2 * part), F32), vmem((slots, part), F32), vmem((slots, part), BF16),
           vmem((slots, 2 * part), BF16)]
        + [vmem((steps, ROWS, quarter), BF16)] * 4 + [vmem((slots // ROWS, ROWS, quarter), BF16)]
        + [vmem((16, share, 3 * part), BF16)] * 2 + [vmem((15, share, 3 * part), BF16)]
        + [vmem((2, tile, part), BF16)] * 2 + [vmem((2, part, tile), BF16)]
        + [dma((steps,))] * 6 + [dma] * 3
        + [dma, dma((16,)), dma((16,)), dma((4,)), dma((4, 15)), dma((width // tile, 5)), dma((2, 3))],
        compiler_params=pltpu.CompilerParams(collective_id=1, has_side_effects=True, vmem_limit_bytes=VMEM_BYTES),
        name="combine_rows",
    )(shadow, upper, lower, s_weight, parts, rows_x, rows_d, w_gate, w_up, w_down)


def shards(tokens, cotangent, expert_ids, gate_weights, shadow_mask, w_gate, w_up, w_down, s_gate, s_up, s_down):
    expert_x, expert_d, shadow_out, shadow_part, upper, lower, s_weight = dispatch_rows(
        tokens, cotangent, expert_ids.T, gate_weights.T, shadow_mask[None, :], s_gate, s_up, s_down.T)
    part = s_gate.shape[1]

    mixed, shadow_sums, grad_gate, grad_up, grad_down = combine_rows(
        shadow_out, upper, lower, s_weight, shadow_part, expert_x, expert_d, w_gate[0], w_up[0], w_down[0])
    grad_gate, grad_up, grad_down = grad_gate[None], grad_up[None], grad_down[None]
    grad_s_gate = shadow_sums[:, :part]
    grad_s_up = shadow_sums[:, part:2 * part]
    grad_s_down = shadow_sums[:, 2 * part:].T

    return mixed, grad_gate, grad_up, grad_down, grad_s_gate, grad_s_up, grad_s_down


def solution(mesh):
    return jax.shard_map(
        shards, mesh=mesh,
        in_specs=(P("ep", "tp"), P("ep", "tp"), P("ep", None), P("ep", None), P("ep"), P("ep", None, "tp"),
                  P("ep", None, "tp"), P("ep", "tp", None), P("ep", "tp"), P("ep", "tp"), P("tp", "ep")),
        out_specs=(P("ep", "tp"), P("ep", None, "tp"), P("ep", None, "tp"), P("ep", "tp", None), P("ep", "tp"),
                   P("ep", "tp"), P("tp", "ep")),
        check_vma=False)
```

```python
import jax
import jax.numpy as jnp
from jax import lax
from jax.experimental import pallas as pl
from jax.experimental.pallas import tpu as pltpu
from jax.sharding import PartitionSpec as P

SLOTS = 16
MIX = 13
ROWS = 64
CUTS = (0, 48, 80, 128, 160)
ORDER = sorted(((j, i) for j in range(4) for i in range(4) if j + i > 0), key=lambda ji: (ji[0] + ji[1], -ji[0]))
FIRST_LEG, E_START, W_PER = 10, 4, 1
VMEM_BYTES = 62 * 1024 * 1024
A_LEAD, A_RATE, R_START, R_RATE, R_MID = 16, 4, 2, 2, 28
B_AT = 14
ANY = pl.BlockSpec(memory_space=pl.ANY)
VMEM = pl.BlockSpec(memory_space=pltpu.VMEM)
MESH = pl.DeviceIdType.MESH
BF16, F32 = jnp.bfloat16, jnp.float32


def contract_rows(left, right):
    return lax.dot_general(left, right, (((0,), (0,)), ((), ())), preferred_element_type=F32)


def split_parts(values):
    upper = values.astype(BF16)
    return upper, (values - upper.astype(F32)).astype(BF16)


def ep_peer(ep, k, sign):
    k = (k * MIX) % 32
    z, y, c = ep // 8, (ep // 2) % 4, ep % 2
    dz, dy, dc = k // 8, (k // 2) % 4, k % 2
    return ((z + sign * dz + 4) % 4) * 8 + ((y + sign * dy + 4) % 4) * 2 + (c + dc) % 2


def drain(ref, sem):
    pltpu.make_async_copy(ref, ref, sem).wait()


def route(ids, gates, mask, disp, gate, s_weight, upper, lower):
    count, slots = disp.shape[1], disp.shape[0]
    experts = slots // SLOTS
    expert = lax.broadcasted_iota(jnp.int32, (experts, count), 0)
    picked = jnp.zeros((experts, count), F32)
    given = jnp.zeros((experts, count), F32)
    for j in range(ids.shape[0]):
        hit = expert == ids[j:j + 1, :]
        picked = picked + jnp.where(hit, 1.0, 0.0)
        given = given + jnp.where(hit, gates[j:j + 1, :], 0.0)
    first = lax.broadcasted_iota(jnp.int32, (count, count), 0)
    second = lax.broadcasted_iota(jnp.int32, (count, count), 1)
    earlier = jnp.where(first < second, 1.0, 0.0).astype(BF16)
    rank = jnp.dot(picked.astype(BF16), earlier, preferred_element_type=F32)
    slot = lax.broadcasted_iota(jnp.int32, (slots, experts), 0)
    owner = lax.broadcasted_iota(jnp.int32, (slots, experts), 1)
    spread = jnp.where(slot // SLOTS == owner, 1.0, 0.0).astype(BF16)

    def widen(values):
        return jnp.dot(spread, values.astype(BF16), preferred_element_type=F32)

    place = (lax.broadcasted_iota(jnp.int32, (slots, count), 0) % SLOTS).astype(F32)
    filled = jnp.where((widen(picked) > 0.5) & (widen(rank) == place), 1.0, 0.0)
    top, rest = split_parts(given)
    middle, last = split_parts(given - top.astype(F32) - rest.astype(F32))
    weight = filled * ((widen(top) + widen(rest)) + widen(middle))
    disp[...] = filled.astype(BF16)
    gate[...] = jnp.sum(weight, axis=1, keepdims=True)
    upper[...], lower[...] = split_parts(weight)
    shadow = gates[ids.shape[0]:ids.shape[0] + 1, :] * mask[...].astype(F32)
    s_weight[...] = jnp.sum(jnp.where(first == second, shadow, 0.0), axis=1, keepdims=True)


def dispatch_kernel(tok, cot, ids, gates, mask, s_gate, s_up, s_down, out_x, out_d, out_s, out_g, upper, lower, s_weight,
                    disp, gate, full_x, full_d, rows_x, rows_d, rows2_x, rows2_d, s_all, acc, hidden, slopes, stage, ring_send, ring_recv, own_sem,
                    a_send, a_recv, b_send, b_recv, f_send, f_recv, w_send, w_recv, pair_send, pair_recv, g_sem):
    tp, ep = lax.axis_index("tp"), lax.axis_index("ep")
    z, y, c = ep // 8, (ep // 2) % 4, ep % 2
    quarter, part, share = tok.shape[1], s_gate.shape[1], s_gate.shape[0]
    mine = pl.multiple_of(tp * quarter, quarter)
    opposite = pl.multiple_of(((tp + 2) % 4) * quarter, quarter)
    my_rows = pl.multiple_of(ep * SLOTS, SLOTS)
    partner = ep + 1 - 2 * c

    barrier = pltpu.get_barrier_semaphore()
    for d in (1, 2, 3):
        pl.semaphore_signal(barrier, inc=1, device_id=((tp + d) % 4, ep), device_id_type=MESH)

    def greet(k, carry):
        pl.semaphore_signal(barrier, inc=1, device_id=(tp, ep_peer(ep, k, 1)), device_id_type=MESH)
        return carry

    lax.fori_loop(1, 32, greet, 0)
    my_share = pl.ds(pl.multiple_of(ep * share, share), share)
    local = [pltpu.make_async_copy(src, s_all.at[my_share, pl.ds(i * part, part)], own_sem.at[i])
             for i, src in enumerate((s_gate, s_up, s_down))]
    local += [pltpu.make_async_copy(tok, full_x.at[:, pl.ds(mine, quarter)], own_sem.at[3]),
              pltpu.make_async_copy(cot, full_d.at[:, pl.ds(mine, quarter)], own_sem.at[4])]
    for copy in local:
        copy.start()
    pl.semaphore_wait(barrier, 34)

    ring = []
    for d in (2, 1, 3):
        for i, (src, full) in enumerate(((tok, full_x), (cot, full_d))):
            copy = pltpu.make_async_remote_copy(
                src_ref=src, dst_ref=full.at[:, pl.ds(mine, quarter)],
                send_sem=ring_send.at[d - 1, i], recv_sem=ring_recv.at[d - 1, i],
                device_id=((tp + d) % 4, ep), device_id_type=MESH)
            copy.start()
            ring.append(copy)

    def colour_step(q, at_first, at_second):
        sign = (1 - 2 * c) * (1 if q % 2 == 0 else -1)
        dz, dy = (at_second, at_first) if q < 2 else (at_first, at_second)
        return ((z + sign * dz + 8) % 4) * 8 + ((y + sign * dy + 8) % 4) * 2 + c

    def pass_on(q, j, i):
        origin = colour_step(q, -j, -i)
        where = s_all.at[pl.ds(pl.multiple_of(origin * share + CUTS[q], 16), CUTS[q + 1] - CUTS[q]), :]
        hops = []
        if i == 0 and j < 3:
            hops.append((colour_step(q, 1, 0), w_send.at[q], w_recv.at[q, (j + 1) * 4]))
        if i < 3:
            hops.append((colour_step(q, 0, 1), w_send.at[q], w_recv.at[q, j * 4 + i + 1]))
        hops.append((partner, pair_send, pair_recv))
        for peer, send_sem, recv_sem in hops:
            pltpu.make_async_remote_copy(src_ref=where, dst_ref=where, send_sem=send_sem, recv_sem=recv_sem,
                                         device_id=(tp, peer), device_id_type=MESH).start()

    for copy in local[:3]:
        copy.wait()
    for q in range(4):
        pass_on(q, 0, 0)

    def select(column, into_x, into_d):
        def one(r, carry):
            at = pl.ds(pl.multiple_of(r * 128, 128), 128)
            cut = pl.ds(column, quarter)
            into_x[at, :] = jnp.dot(disp[at, :], full_x[:, cut], preferred_element_type=F32).astype(BF16)
            into_d[at, :] = (gate[at, :] * jnp.dot(disp[at, :], full_d[:, cut], preferred_element_type=F32)).astype(BF16)
            return carry
        lax.fori_loop(0, into_x.shape[0] // 128, one, 0)

    def send_rows(first, last, src_x, src_d, column, send_sem, recv_sem):
        def one(k, carry):
            peer = ep_peer(ep, k, 1)
            theirs = pl.multiple_of(peer * SLOTS, SLOTS)
            for src, out in ((src_x, out_x), (src_d, out_d)):
                pltpu.make_async_remote_copy(
                    src_ref=src.at[pl.ds(theirs, SLOTS), :],
                    dst_ref=out.at[pl.ds(my_rows, SLOTS), pl.ds(column, quarter)],
                    send_sem=send_sem, recv_sem=recv_sem, device_id=(tp, peer), device_id_type=MESH).start()
            return carry
        lax.fori_loop(first, last, one, 0)

    def keep_rows(src_x, src_d, column, sems):
        copies = [pltpu.make_async_copy(src.at[pl.ds(my_rows, SLOTS), :],
                                        out.at[pl.ds(my_rows, SLOTS), pl.ds(column, quarter)], own_sem.at[sem])
                  for src, out, sem in ((src_x, out_x, sems), (src_d, out_d, sems + 1))]
        for copy in copies:
            copy.start()
        return copies

    def forward(source):
        at = pl.ds(pl.multiple_of(source * SLOTS, SLOTS), SLOTS), pl.ds(mine, quarter)
        for i, d in enumerate((1, 3)):
            for out in (out_x, out_d):
                pltpu.make_async_remote_copy(
                    src_ref=out.at[at], dst_ref=out.at[at], send_sem=f_send.at[i], recv_sem=f_recv.at[i],
                    device_id=((tp + d) % 4, ep), device_id_type=MESH).start()

    def relay(k, carry=0):
        source = ep_peer(ep, k, -1)
        drain(out_x.at[pl.ds(0, SLOTS), pl.ds(0, 2 * quarter)], a_recv.at[source])
        forward(source)
        return carry

    route(ids, gates, mask, disp, gate, s_weight, upper, lower)
    for copy in local[3:]:
        copy.wait()
    select(mine, rows_x, rows_d)
    kept = keep_rows(rows_x, rows_d, mine, 5)
    sent, relayed = 1, 1
    for r, (j, i) in enumerate(ORDER):
        upto = min(32, A_LEAD + A_RATE * (r + 1))
        if upto > sent:
            send_rows(sent, upto, rows_x, rows_d, mine, a_send, a_recv.at[ep])
            sent = upto
        for q in range(4):
            drain(s_all.at[pl.ds(0, CUTS[q + 1] - CUTS[q]), :], w_recv.at[q, j * 4 + i])
            pass_on(q, j, i)
        if r == 0:
            for copy in kept:
                copy.wait()
            forward(ep)
        if r == B_AT:
            for copy in ring[:2]:
                copy.wait_recv()
            select(opposite, rows2_x, rows2_d)
            send_rows(1, 32, rows2_x, rows2_d, opposite, b_send, b_recv)
            kept = keep_rows(rows2_x, rows2_d, opposite, 7)
        if r >= R_START:
            lax.fori_loop(relayed, relayed + R_RATE, relay, 0)
            relayed += R_RATE

    for copy in ring[2:]:
        copy.wait_recv()
    lax.fori_loop(relayed, R_MID, relay, 0)
    drain(s_all.at[pl.ds(0, s_all.shape[0] // 2), :], pair_recv)

    tile = 640
    tiles = full_x.shape[1] // tile
    left = (32 - R_MID) // tiles
    acc[...] = jnp.zeros_like(acc)

    def before(t, carry):
        at = pl.ds(pl.multiple_of(t * tile, tile), tile)
        full_d[:, at] = (s_weight[...] * full_d[:, at].astype(F32)).astype(BF16)
        acc[:, :2 * part] += jnp.dot(full_x[:, at], s_all[at, :2 * part], preferred_element_type=F32)
        acc[:, 2 * part:] += jnp.dot(full_d[:, at], s_all[at, 2 * part:], preferred_element_type=F32)
        lax.fori_loop(R_MID + t * left, R_MID + (t + 1) * left, relay, 0)
        return carry

    lax.fori_loop(0, tiles, before, 0)
    lax.fori_loop(R_MID + tiles * left, 32, relay, 0)
    pre_gate, pre_up, grad = acc[:, :part], acc[:, part:2 * part], acc[:, 2 * part:]
    sigmoid = jax.nn.sigmoid(pre_gate)
    active = pre_gate * sigmoid
    hidden[...] = (active * pre_up).astype(BF16)
    slopes[:, :part] = (grad * pre_up * sigmoid * (1.0 + pre_gate * (1.0 - sigmoid))).astype(BF16)
    slopes[:, part:] = (grad * active).astype(BF16)

    def after(t, carry):
        at = pl.ds(pl.multiple_of(t * tile, tile), tile)
        slot = t % 2
        result = pltpu.make_async_copy(stage.at[slot], out_g.at[at, :], g_sem.at[slot])

        @pl.when(t >= 2)
        def _():
            result.wait()

        out_s[:, at] = lax.dot_general(hidden[...], s_all[at, 2 * part:], (((1,), (1,)), ((), ())),
                                       preferred_element_type=F32).astype(BF16)
        stage[slot, :, :2 * part] = contract_rows(full_x[:, at], slopes[...]).astype(BF16)
        stage[slot, :, 2 * part:] = contract_rows(full_d[:, at], hidden[...]).astype(BF16)
        result.start()
        return carry

    lax.fori_loop(0, tiles, after, 0)
    for slot in range(2):
        drain(stage.at[slot], g_sem.at[slot])

    for copy in kept:
        copy.wait()
    for copy in ring:
        copy.wait_send()
    for q in range(4):
        drain(s_all.at[pl.ds(0, 15 * (CUTS[q + 1] - CUTS[q])), :], w_send.at[q])
    drain(s_all.at[pl.ds(0, s_all.shape[0] // 2), :], pair_send)
    others = out_x.at[pl.ds(0, 31 * SLOTS), pl.ds(0, 2 * quarter)]
    everything = out_x.at[:, pl.ds(0, 2 * quarter)]
    drain(others, a_send)
    drain(others, b_send)
    drain(others, b_recv)
    for i in range(2):
        drain(everything, f_send.at[i])
        drain(everything, f_recv.at[i])


def dispatch_rows(tok, cot, ids, gates, mask, s_gate, s_up, s_down):
    count, quarter = tok.shape
    slots, part = 32 * SLOTS, s_gate.shape[1]
    width = 4 * quarter
    dma = pltpu.SemaphoreType.DMA
    vmem = pltpu.VMEM
    return pl.pallas_call(
        dispatch_kernel,
        out_shape=(jax.ShapeDtypeStruct((slots, width), BF16),) * 2
        + (jax.ShapeDtypeStruct((count, width), BF16), jax.ShapeDtypeStruct((width, 3 * part), BF16))
        + (jax.ShapeDtypeStruct((slots, count), BF16),) * 2 + (jax.ShapeDtypeStruct((count, 1), F32),),
        in_specs=[VMEM] * 8,
        out_specs=(ANY, ANY, VMEM, ANY, VMEM, VMEM, VMEM),
        scratch_shapes=[vmem((slots, count), BF16), vmem((slots, 1), F32)] + [vmem((count, width), BF16)] * 2 + [vmem((slots, quarter), BF16)] * 4
        + [vmem((width, 3 * part), BF16), vmem((count, 3 * part), F32), vmem((count, part), BF16),
           vmem((count, 2 * part), BF16), vmem((2, 640, 3 * part), BF16)]
        + [dma((3, 2)), dma((3, 2)), dma((9,)), dma, dma((32,)), dma, dma, dma((2,)), dma((2,)), dma((4,)), dma((4, 16)),
           dma, dma, dma((2,))],
        compiler_params=pltpu.CompilerParams(collective_id=0, has_side_effects=True),
        name="dispatch_rows",
    )(tok, cot, ids, gates, mask, s_gate, s_up, s_down)


def combine_kernel(shadow, upper, lower, s_weight, parts, rows_x, rows_d, w_gate, w_up, w_down, mixed, share_out,
                   grad_gate, grad_up, grad_down, back, shadow_sum, routed, all_x, all_d, down, strip, acc, acc_grad,
                   hidden, slopes, passing, relayed, far, near, total, held, pair, arrived, put_gate, put_up,
                   put_down, pass_send, pass_recv, far_send, far_recv, near_send, near_recv, back_send,
                   back_recv, own_sem, pair_send, pair_recv, held_sem, s_send, s_recv, load_sem, put_sem):
    tp, ep = lax.axis_index("tp"), lax.axis_index("ep")
    z, y, c = ep // 8, (ep // 2) % 4, ep % 2
    quarter = back.shape[1]
    blocks = routed.shape[0] // ROWS
    steps = blocks + shadow.shape[0] // ROWS
    per = ROWS // SLOTS
    share = share_out.shape[0]
    tile, part = strip.shape[1], hidden.shape[1]
    tiles = rows_x.shape[1] // tile
    early = steps - blocks

    barrier = pltpu.get_barrier_semaphore()
    for d in (1, 3):
        pl.semaphore_signal(barrier, inc=1, device_id=((tp + d) % 4, ep), device_id_type=MESH)

    def greet(k, carry):
        pl.semaphore_signal(barrier, inc=1, device_id=(tp, ep_peer(ep, k, 1)), device_id_type=MESH)
        return carry

    lax.fori_loop(1, 32, greet, 0)

    def share_rows(chip, core):
        return parts.at[pl.ds(pl.multiple_of((chip * 2 + core) * share, share), share), :]

    def chip_at(k):
        return ((z + k // 4) % 4) * 4 + (y + k % 4) % 4

    def columns_of(t):
        return pl.ds(t * tile, tile)

    def loads(t):
        at, sem = columns_of(t), load_sem.at[t]
        return [pltpu.make_async_copy(src.at[:, at], dst.at[:, at], sem.at[i])
                for i, (src, dst) in enumerate(((rows_x, all_x), (rows_d, all_d), (w_down, down)))]

    def strips(t):
        return [pltpu.make_async_copy(src.at[columns_of(t), :], strip.at[t % 2, :, pl.ds(i * part, part)],
                                      load_sem.at[t, 3 + i]) for i, src in enumerate((w_gate, w_up))]

    for t in range(tiles):
        for copy in (loads(t) if t < 3 else []) + (strips(t) if t < 2 else []):
            copy.start()

    def take(k, carry):
        chip = chip_at(k)
        pltpu.make_async_copy(share_rows(chip, c), held.at[chip], held_sem.at[chip]).start()
        return carry

    lax.fori_loop(0, 16, take, 0)
    pl.semaphore_wait(barrier, 33)

    def swap(k, carry):
        chip = chip_at(k)
        pltpu.make_async_remote_copy(
            src_ref=share_rows(chip, 1 - c), dst_ref=pair.at[chip], send_sem=pair_send, recv_sem=pair_recv.at[chip],
            device_id=(tp, ep + 1 - 2 * c), device_id_type=MESH).start()
        return carry

    lax.fori_loop(0, 16, swap, 0)

    def block(i):
        return (i + ep // per) % blocks

    def piece(i, owner):
        columns = pl.ds(pl.multiple_of((owner % 4) * quarter, quarter), quarter)
        if i >= early:
            return routed.at[pl.ds(pl.multiple_of(block(i) * ROWS, ROWS), ROWS), columns]
        return shadow.at[pl.ds(i * ROWS, ROWS), columns]

    def way(i):
        return 1 if i % 2 == 0 else 3

    def send(src, dst, sems, i, d):
        return pltpu.make_async_remote_copy(
            src_ref=src, dst_ref=dst.at[i], send_sem=sems[0].at[i], recv_sem=sems[1].at[i],
            device_id=((tp + d) % 4, ep), device_id_type=MESH)

    passes = [send(piece(i, tp + 2), passing, (pass_send, pass_recv), i, way(i)) for i in range(steps)]
    nears = [send(piece(i, tp + 4 - way(i)), near, (near_send, near_recv), i, 4 - way(i)) for i in range(steps)]
    fars = [send(relayed.at[i], far, (far_send, far_recv), i, way(i)) for i in range(steps)]

    def finish(i):
        fars[i].wait_recv()
        nears[i].wait_recv()
        result = piece(i, tp)[...].astype(F32) + far[i].astype(F32) + near[i].astype(F32)
        if i < early:
            shadow_sum[pl.ds(i * ROWS, ROWS), :] = result
            return
        total[i - early] = result.astype(BF16)
        for j in range(per):
            peer = block(i) * per + j
            source = total.at[i - early, pl.ds(j * SLOTS, SLOTS), :]
            target = back.at[pl.ds(pl.multiple_of(ep * SLOTS, SLOTS), SLOTS), :]

            @pl.when(peer != ep)
            def _():
                pltpu.make_async_remote_copy(src_ref=source, dst_ref=target, send_sem=back_send, recv_sem=back_recv,
                                             device_id=(tp, peer), device_id_type=MESH).start()

            @pl.when(peer == ep)
            def _():
                pltpu.make_async_copy(source, target, own_sem).start()

    def relay(i):
        passes[i].wait_recv()
        relayed[i] = (piece(i, tp + way(i))[...].astype(F32) + passing[i].astype(F32)).astype(BF16)
        fars[i].start()
        if i >= early:
            nears[i].start()

    def ahead(t):
        for copy in loads(t) + strips(t):
            copy.wait()
        acc[...] += jnp.dot(all_x[:, columns_of(t)], strip[t % 2], preferred_element_type=F32)
        acc_grad[...] += lax.dot_general(all_d[:, columns_of(t)], down[:, columns_of(t)], (((1,), (1,)), ((), ())),
                                         preferred_element_type=F32)
        if t + 2 < tiles:
            for copy in strips(t + 2):
                copy.start()
        if t + 3 < tiles:
            for copy in loads(t + 3):
                copy.start()

    def activate():
        pre_gate, pre_up, grad = acc[:, :part], acc[:, part:], acc_grad[...]
        sigmoid = jax.nn.sigmoid(pre_gate)
        active = pre_gate * sigmoid
        hidden[...] = (active * pre_up).astype(BF16)
        slopes[:, :part] = (grad * pre_up * sigmoid * (1.0 + pre_gate * (1.0 - sigmoid))).astype(BF16)
        slopes[:, part:] = (grad * active).astype(BF16)

    def project(owner):
        at = pl.ds(pl.multiple_of((owner % 4) * quarter, quarter), quarter)
        routed[:, at] = jnp.dot(hidden[...], down[:, at], preferred_element_type=F32).astype(BF16)

    def puts(t):
        slot = t % 2
        return [pltpu.make_async_copy(put_gate.at[slot], grad_gate.at[columns_of(t), :], put_sem.at[slot, 0]),
                pltpu.make_async_copy(put_up.at[slot], grad_up.at[columns_of(t), :], put_sem.at[slot, 1]),
                pltpu.make_async_copy(put_down.at[slot], grad_down.at[:, columns_of(t)], put_sem.at[slot, 2])]

    def weights(t):
        slot = t % 2
        if t >= 2:
            for copy in puts(t - 2):
                copy.wait()
        both = contract_rows(all_x[:, columns_of(t)], slopes[...]).astype(BF16)
        put_gate[slot], put_up[slot] = both[:, :part], both[:, part:]
        put_down[slot] = contract_rows(hidden[...], all_d[:, columns_of(t)]).astype(BF16)
        for copy in puts(t):
            copy.start()

    def colour_step(q, at_first, at_second):
        sign = (1 - 2 * c) * (1 if q % 2 == 0 else -1)
        dz, dy = (at_second, at_first) if q < 2 else (at_first, at_second)
        return ((z + sign * dz + 8) % 4) * 4 + (y + sign * dy + 8) % 4

    def mine(q, a, b):
        return held.at[colour_step(q, -a, -b), pl.ds(CUTS[q], CUTS[q + 1] - CUTS[q]), :]

    def hand_on(q, a, b, along_first, event):
        peer = colour_step(q, 1, 0) if along_first else colour_step(q, 0, 1)
        pltpu.make_async_remote_copy(
            src_ref=mine(q, a, b), dst_ref=arrived.at[event, pl.ds(CUTS[q], CUTS[q + 1] - CUTS[q]), :],
            send_sem=s_send.at[q], recv_sem=s_recv.at[q, event], device_id=(tp, peer * 2 + c),
            device_id_type=MESH).start()

    def gather(q, a, b, event):
        rows = pl.ds(CUTS[q], CUTS[q + 1] - CUTS[q])
        drain(arrived.at[event, rows, :], s_recv.at[q, event])
        kept = mine(q, a, b)
        kept[...] = (kept[...].astype(F32) + arrived[event, rows, :].astype(F32)).astype(BF16)

    def first_leg(t, b):
        for q in range(4):
            gather(q, (t + 1) % 4, b, (t - 1) * 4 + b)
            if t < 3:
                hand_on(q, t + 1, b, True, t * 4 + b)
            elif b == 1:
                hand_on(q, 0, 1, False, 12)

    def second_leg(t):
        for q in range(4):
            gather(q, 0, (t + 1) % 4, 11 + t)
            if t < 3:
                hand_on(q, 0, t + 1, False, 12 + t)

    def join(k, carry):
        chip = chip_at(k)
        drain(held.at[chip], held_sem.at[chip])
        drain(pair.at[chip], pair_recv.at[chip])
        held[chip] = (held[chip].astype(F32) + pair[chip].astype(F32)).astype(BF16)
        return carry

    for i in range(early):
        passes[i].start()
    for i in range(early):
        nears[i].start()
    for ref in (acc, acc_grad):
        ref[...] = jnp.zeros_like(ref)
    plan = [lambda t=t, b=b: first_leg(t, b) for t in (1, 2, 3) for b in (1, 2, 3, 0)]
    plan = plan[:10] + [lambda: second_leg(1), plan[10], lambda: second_leg(2), plan[11], lambda: second_leg(3)]
    for t in range(tiles):
        if t >= 2:
            lax.fori_loop(2 * t - 4, 2 * t - 2, join, 0)
        if t == tiles - 1:
            for b in (1, 2, 3, 0):
                for q in range(4):
                    hand_on(q, 1, b, True, b)
            for i in range(early):
                relay(i)
        ahead(t)
        if t >= FIRST_LEG and plan:
            plan.pop(0)()
    activate()
    project(tp + 2)
    for i in range(early, steps):
        passes[i].start()
    project(tp + 1)
    project(tp + 3)
    project(tp)
    for i in range(early):
        finish(i)
    todo = [lambda i=i: relay(i) for i in range(early, steps)]
    ends = [lambda i=i: finish(i) for i in range(early, steps)]
    work = [lambda t=t: weights(t) for t in range(tiles)]
    while plan or todo or ends or work:
        for queue, count in ((work, W_PER), (plan, 1), (todo, 1)):
            for one in queue[:count]:
                one()
            del queue[:count]
        if len(plan) < E_START and len(todo) < len(ends):
            ends.pop(0)()
    final = pltpu.make_async_copy(held.at[z * 4 + y], share_out, own_sem)

    for i in range(steps):
        passes[i].wait_send()
        nears[i].wait_send()
        fars[i].wait_send()
    drain(back.at[pl.ds(0, SLOTS), :], own_sem)
    final.start()
    final.wait()
    for copy in puts(tiles - 2) + puts(tiles - 1):
        copy.wait()
    drain(held, pair_send)
    for q in range(4):
        drain(parts.at[pl.ds(0, 15 * (CUTS[q + 1] - CUTS[q])), :], s_send.at[q])
    drain(back.at[pl.ds(0, 31 * SLOTS), :], back_send)
    drain(back.at[pl.ds(0, 31 * SLOTS), :], back_recv)
    result = contract_rows(upper[...], back[...]) + contract_rows(lower[...], back[...])
    mixed[...] = (result + s_weight[...] * shadow_sum[...]).astype(BF16)


def combine_rows(shadow, upper, lower, s_weight, parts, rows_x, rows_d, w_gate, w_up, w_down):
    (slots, width), (count, _) = rows_x.shape, shadow.shape
    quarter, part, share, steps, tile = width // 4, w_gate.shape[1], width // 32, (slots + count) // ROWS, 512
    dma, vmem, like = pltpu.SemaphoreType.DMA, pltpu.VMEM, jax.ShapeDtypeStruct
    return pl.pallas_call(
        combine_kernel,
        out_shape=(like((count, quarter), BF16), like((share, 3 * part), BF16),
                   like((width, part), BF16), like((width, part), BF16), like((part, width), BF16)),
        in_specs=[VMEM] * 4 + [ANY] * 6,
        out_specs=(VMEM, VMEM, ANY, ANY, ANY),
        scratch_shapes=[vmem((slots, quarter), BF16), vmem((count, quarter), F32)]
        + [vmem((slots, width), BF16)] * 3 + [vmem((part, width), BF16), vmem((2, tile, 2 * part), BF16)]
        + [vmem((slots, 2 * part), F32), vmem((slots, part), F32), vmem((slots, part), BF16),
           vmem((slots, 2 * part), BF16)]
        + [vmem((steps, ROWS, quarter), BF16)] * 4 + [vmem((slots // ROWS, ROWS, quarter), BF16)]
        + [vmem((16, share, 3 * part), BF16)] * 2 + [vmem((15, share, 3 * part), BF16)]
        + [vmem((2, tile, part), BF16)] * 2 + [vmem((2, part, tile), BF16)]
        + [dma((steps,))] * 6 + [dma] * 3
        + [dma, dma((16,)), dma((16,)), dma((4,)), dma((4, 15)), dma((width // tile, 5)), dma((2, 3))],
        compiler_params=pltpu.CompilerParams(collective_id=1, has_side_effects=True, vmem_limit_bytes=VMEM_BYTES),
        name="combine_rows",
    )(shadow, upper, lower, s_weight, parts, rows_x, rows_d, w_gate, w_up, w_down)


def settle_kernel(*refs):
    for src, dst in zip(refs[:4], refs[4:]):
        dst[...] = src[...]


def settle(mixed, grad_gate, grad_up, grad_down):
    (count, quarter), (width, part) = mixed.shape, grad_gate.shape
    steps = 5
    tall = pl.BlockSpec((width // steps, part), lambda i: (i, 0))
    specs = [pl.BlockSpec((count, quarter // steps), lambda i: (0, i)), tall, tall,
             pl.BlockSpec((part, width // steps), lambda i: (0, i))]
    arrays = (mixed, grad_gate, grad_up, grad_down)
    return pl.pallas_call(
        settle_kernel, grid=(steps,), out_shape=tuple(jax.ShapeDtypeStruct(a.shape, a.dtype) for a in arrays),
        in_specs=specs, out_specs=tuple(specs), name="settle")(*arrays)


def shards(tokens, cotangent, expert_ids, gate_weights, shadow_mask, w_gate, w_up, w_down, s_gate, s_up, s_down):
    expert_x, expert_d, shadow_out, shadow_part, upper, lower, s_weight = dispatch_rows(
        tokens, cotangent, expert_ids.T, gate_weights.T, shadow_mask[None, :], s_gate, s_up, s_down.T)
    part = s_gate.shape[1]

    mixed, shadow_sums, grad_gate, grad_up, grad_down = combine_rows(
        shadow_out, upper, lower, s_weight, shadow_part, expert_x, expert_d, w_gate[0], w_up[0], w_down[0])
    mixed, grad_gate, grad_up, grad_down = settle(mixed, grad_gate, grad_up, grad_down)
    grad_gate, grad_up, grad_down = grad_gate[None], grad_up[None], grad_down[None]
    grad_s_gate = shadow_sums[:, :part]
    grad_s_up = shadow_sums[:, part:2 * part]
    grad_s_down = shadow_sums[:, 2 * part:].T

    return mixed, grad_gate, grad_up, grad_down, grad_s_gate, grad_s_up, grad_s_down


def solution(mesh):
    return jax.shard_map(
        shards, mesh=mesh,
        in_specs=(P("ep", "tp"), P("ep", "tp"), P("ep", None), P("ep", None), P("ep"), P("ep", None, "tp"),
                  P("ep", None, "tp"), P("ep", "tp", None), P("ep", "tp"), P("ep", "tp"), P("tp", "ep")),
        out_specs=(P("ep", "tp"), P("ep", None, "tp"), P("ep", None, "tp"), P("ep", "tp", None), P("ep", "tp"),
                   P("ep", "tp"), P("tp", "ep")),
        check_vma=False)
```
